128 devices in a mesh: row: 8 (over z, core), col: 16 (over y, x).
Axes of the slice: x: 4, y: 4, z: 4, core: 2. Of those that a mesh axis runs over, the one named last changes fastest.
Arguments:
- symmetric: float32 [16384, 16384], P('row', 'col'), may hold values from -8 to 8, as said below
- reflectors: float32 [4, 64, 16384], P(None, None, ('row', 'col')), may hold values from -0.125 to 0.125
- tri_factor: float32 [4, 64, 64], replicated, may hold values from -0.4 to 1.5, as said below
Outputs:
- updated: float32 [16384, 16384], P('row', 'col')
The draws below stay inside these ranges and needn't reach their ends.
Inputs may be any that keep to these rules, and one draw needn't show every extreme that they name: symmetric is a symmetric matrix. Each tri_factor[p] is upper triangular.
All inputs are finite; a program needn't handle non-finite values.
Results may differ from the reference program's by a relative error of at most 0.00029.
Values sent between devices are 32-bit elements; how exact they have to be, the bound alone decides.
A program may use at most 64 MiB of HBM per device.

```python
import jax
import jax.numpy as jnp
from jax import lax

N = 16384
NB = 64
PANELS = 4


def draw_symmetric(key, part):
    base = jax.random.normal(key, (N, N), jnp.float32)
    paired = (base + base.T) * 0.70710678
    return jnp.clip(paired, -8.0, 8.0)


def draw_tri_factor(key, part):
    first = jax.random.fold_in(key, 11)
    second = jax.random.fold_in(key, 13)
    diagonal = jax.random.uniform(first, (PANELS, NB), jnp.float32, 0.6, 1.4)
    spread = jnp.clip(0.1 * jax.random.normal(second, (PANELS, NB, NB), jnp.float32), -0.4, 0.4)
    return jnp.triu(spread, 1) + diagonal[:, :, None] * jnp.eye(NB, dtype=jnp.float32)[None, :, :]


def block_levels(stream_key, dims, pieces, low, largest):
    def one(position, blocks):
        heights = jax.random.uniform(jax.random.fold_in(jax.random.fold_in(stream_key, 6), position), (blocks,), jnp.float32, low / len(pieces), largest / len(pieces))
        return jnp.repeat(jnp.exp(heights), dims[position] // blocks).reshape((-1,) + (1,) * (len(dims) - position - 1))

    gain = one(*pieces[0])
    for cut in pieces[1:]:
        gain = gain * one(*cut)
    return gain


def noise(rng, extent, scale, most, split=(), held_as=jnp.bfloat16):
    factor_of = block_levels(rng, extent, split, -0.22, 0.18) if split else 1.0
    drawn = jax.random.normal(rng, extent, jnp.float32) * scale * factor_of
    return jnp.minimum(jnp.maximum(drawn, -most), most).astype(held_as)


def setup_inputs(seed: int = 0) -> dict:
    key_of = jax.random.split(jax.random.key(seed), 4)
    symmetric = draw_symmetric(jax.random.fold_in(key_of[3], 71), 0)
    reflectors = noise(key_of[1], (PANELS, NB, N), (N // 8) ** -0.5, 0.125, ((2, 128),), jnp.float32)
    tri_factor = draw_tri_factor(jax.random.fold_in(key_of[3], 71), 0)
    return {"symmetric": symmetric, "reflectors": reflectors, "tri_factor": tri_factor}


def reference(symmetric, reflectors, tri_factor):
    highest = lax.Precision.HIGHEST
    matrix = symmetric
    for panel in range(PANELS):
        reflect = reflectors[panel]
        factor = tri_factor[panel]
        product = lax.dot_general(reflect, matrix, (((1,), (1,)), ((), ())), precision=highest, preferred_element_type=jnp.float32)
        image = jnp.dot(factor.T, product, precision=highest, preferred_element_type=jnp.float32)
        inner = lax.dot_general(reflect, image, (((1,), (1,)), ((), ())), precision=highest, preferred_element_type=jnp.float32)
        coupling = jnp.dot(factor.T, inner, precision=highest, preferred_element_type=jnp.float32)
        update = image - 0.5 * jnp.dot(coupling.T, reflect, precision=highest, preferred_element_type=jnp.float32)
        left_block = jnp.concatenate([reflect, update], axis=0)
        right_block = jnp.concatenate([update, reflect], axis=0)
        matrix = matrix - lax.dot_general(left_block, right_block, (((0,), (0,)), ((), ())), precision=highest, preferred_element_type=jnp.float32)
    return matrix
```

```python
import functools

import jax
import jax.numpy as jnp
from jax import lax
from jax.experimental import pallas as pl
from jax.experimental.pallas import tpu as pltpu
from jax.sharding import PartitionSpec as P

MESH = pl.DeviceIdType.MESH
F32 = jnp.float32
BF16 = jnp.bfloat16
NN = (((1,), (0,)), ((), ()))
NT = (((1,), (1,)), ((), ()))
TN = (((0,), (0,)), ((), ()))


def split(value):
    high = value.astype(BF16)
    return high, (value - high.astype(F32)).astype(BF16)


def dot3(left, right, dims):
    (lh, ll), (rh, rl) = left, right
    dot = functools.partial(lax.dot_general, dimension_numbers=dims, preferred_element_type=F32)
    return dot(lh, rh) + dot(lh, rl) + dot(ll, rh)


def dotf(left, right, dims):
    return dot3(split(left), split(right), dims)


class Place:
    def __init__(self):
        row, col = lax.axis_index("row"), lax.axis_index("col")
        self.z, self.k = row // 2, lax.rem(row, 2)
        self.y, self.x = col // 4, lax.rem(col, 4)
        self.s = row

    def dev(self, z=None, k=None, y=None, x=None):
        z = self.z if z is None else z
        k = self.k if k is None else k
        y = self.y if y is None else y
        x = self.x if x is None else x
        return (z * 2 + k, y * 4 + x)

    def out_v(self):
        s = lax.rem(self.y, 2) * 4 + self.x
        return self.dev(s // 2, lax.rem(s, 2), self.z, self.k * 2 + self.y // 2), s

    def out_y(self):
        half = lax.rem(self.x, 2)
        b = half * 8 + self.s
        return self.dev(self.y, self.x // 2, b // 4, lax.rem(b, 4)), b


def wrap(value, by):
    return lax.rem(value + by + 4, 4)


class Ring:
    def __init__(self, ssem, rsem):
        self.ssem, self.rsem = ssem, rsem
        self.sent = []

    def copy(self, i, src, dst, dev):
        return pltpu.make_async_remote_copy(
            src_ref=src, dst_ref=dst, send_sem=self.ssem.at[i], recv_sem=self.rsem.at[i],
            device_id=dev, device_id_type=MESH)

    def send(self, i, src, dst, dev):
        c = self.copy(i, src, dst, dev)
        c.start()
        self.sent.append(c)

    def got(self, i, ref, dev):
        self.copy(i, ref, ref, dev).wait_recv()

    def drain(self):
        for c in self.sent:
            c.wait_send()
        self.sent = []


def plane_gather(pos, buf, ssem, rsem, hooks=()):
    ring = Ring(ssem, rsem)
    rows = buf.shape[1]
    half, quarter = rows // 2, rows // 4
    me = pos.dev()

    class Half:
        def __init__(self, h):
            self.h, self.base = h, h * 20
            self.i, self.j = (pos.x, pos.y) if h == 0 else (pos.y, pos.x)

        def at(self, di, dj, part=None):
            i, j = wrap(self.i, di), wrap(self.j, dj)
            slot = j * 4 + i if self.h == 0 else i * 4 + j
            if part is None:
                return buf.at[slot, pl.ds(self.h * half, half)]
            return buf.at[slot, pl.ds(self.h * half + part * quarter, quarter)]

        def first(self, d):
            return pos.dev(x=wrap(pos.x, d)) if self.h == 0 else pos.dev(y=wrap(pos.y, d))

        def second(self, d):
            return pos.dev(y=wrap(pos.y, d)) if self.h == 0 else pos.dev(x=wrap(pos.x, d))

        def send1(self):
            for n, d in ((0, 1), (1, -1)):
                ring.send(self.base + n, self.at(0, 0), self.at(0, 0), self.first(d))

        def relay1(self, n):
            d = (-1, 1)[n]
            ring.got(self.base + n, self.at(d, 0), me)
            ref = self.at(d, 0, n)
            ring.send(self.base + 2 + n, ref, ref, self.first(-d))

        def far1(self):
            for n in (0, 1):
                ring.got(self.base + 2 + n, self.at(2, 0, n), me)

        def send2(self, c):
            di = (0, -1, 1, 2)[c]
            for n, d in ((0, 1), (1, -1)):
                ring.send(self.base + 4 + 4 * c + n, self.at(di, 0), self.at(di, 0), self.second(d))

        def relay2(self, c):
            di = (0, -1, 1, 2)[c]
            for n, d in ((0, -1), (1, 1)):
                ring.got(self.base + 4 + 4 * c + n, self.at(di, d), me)
                ref = self.at(di, d, n)
                ring.send(self.base + 4 + 4 * c + 2 + n, ref, ref, self.second(-d))

        def far2(self, c):
            di = (0, -1, 1, 2)[c]
            for n in (0, 1):
                ring.got(self.base + 4 + 4 * c + 2 + n, self.at(di, 2, n), me)

    halves = (Half(0), Half(1))
    for h in halves:
        h.send1()
    for h in halves:
        h.send2(0)
    for h in halves:
        h.relay1(0)
        h.send2(1)
        h.relay1(1)
        h.send2(2)
    for hook in hooks:
        hook()
    for h in halves:
        h.relay2(0)
    for h in halves:
        h.far1()
        h.send2(3)
    for c in (1, 2, 3):
        for h in halves:
            h.relay2(c)
    for c in (0, 1, 2, 3):
        for h in halves:
            h.far2(c)
    return ring


class Column:
    def __init__(self, pos, buf, ssem, rsem):
        self.pos, self.buf = pos, buf
        self.ring = Ring(ssem, rsem)
        self.me = pos.dev()
        self.partner = pos.dev(k=1 - pos.k)
        self.quarter = buf.shape[1] // 2

    def at(self, dz, part=None, other=False):
        k = 1 - self.pos.k if other else self.pos.k
        slot = wrap(self.pos.z, dz) * 2 + k
        if part is None:
            return self.buf.at[slot]
        return self.buf.at[slot, pl.ds(part * self.quarter, self.quarter)]

    def zdev(self, d):
        return self.pos.dev(z=wrap(self.pos.z, d))

    def start(self):
        own = self.at(0)
        self.ring.send(0, own, own, self.zdev(1))
        self.ring.send(1, own, own, self.zdev(-1))
        self.ring.send(4, own, own, self.partner)

    def relay(self):
        for n, d in ((0, -1), (1, 1)):
            ref = self.at(d)
            self.ring.got(n, ref, self.me)
            part = self.at(d, n)
            self.ring.send(2 + n, part, part, self.zdev(-d))
            self.ring.send(5 + n, ref, ref, self.partner)

    def finish(self):
        for n in (0, 1):
            self.ring.got(2 + n, self.at(2, n), self.me)
        ref = self.at(2)
        self.ring.send(7, ref, ref, self.partner)
        for i, dz in ((4, 0), (5, -1), (6, 1), (7, 2)):
            self.ring.got(i, self.at(dz, other=True), self.me)


class Total:
    def __init__(self, pos, whole, out, part, in1, in2, in3, ssem, rsem):
        self.pos, self.whole, self.out, self.part = pos, whole, out, part
        self.ins = (in1, in2, in3)
        self.ring = Ring(ssem, rsem)
        self.me = pos.dev()
        self.rows = part.shape[0]

    def other(self, d):
        s = lax.rem(self.pos.s + d, 8)
        return s, self.pos.dev(s // 2, lax.rem(s, 2))

    def piece(self, s, ref=None):
        ref = self.whole if ref is None else ref
        return ref.at[pl.ds(pl.multiple_of(s * self.rows, self.rows), self.rows)]

    def step1(self):
        for d in range(1, 8):
            s, dev = self.other(d)
            self.ring.send(d - 1, self.piece(s), self.ins[0].at[d - 1], dev)

    def step2(self):
        value = self.piece(self.pos.s)[...]
        for d in range(7):
            self.ring.got(d, self.ins[0].at[d], self.me)
            value = value + self.ins[0][d]
        self.part[...] = value
        for d in (1, 2, 3):
            self.ring.send(6 + d, self.part, self.ins[1].at[d - 1], self.pos.dev(x=wrap(self.pos.x, d)))

    def step3(self):
        value = self.part[...]
        for d in (1, 2, 3):
            self.ring.got(6 + d, self.ins[1].at[d - 1], self.me)
            value = value + self.ins[1][d - 1]
        mid = self.ins[2].at[3]
        mid[...] = value
        for d in (1, 2, 3):
            self.ring.send(9 + d, mid, self.ins[2].at[d - 1], self.pos.dev(y=wrap(self.pos.y, d)))

    def step4(self):
        value = self.ins[2][3]
        for d in (1, 2, 3):
            self.ring.got(9 + d, self.ins[2].at[d - 1], self.me)
            value = value + self.ins[2][d - 1]
        own = self.piece(self.pos.s, self.out)
        own[...] = value
        for d in range(1, 8):
            _, dev = self.other(d)
            self.ring.send(12 + d, own, own, dev)

    def finish(self):
        for d in range(1, 8):
            s, _ = self.other(8 - d)
            self.ring.got(12 + d, self.piece(s, self.out), self.me)
        self.ring.drain()


def exchange(dev, me, src, dst, ssem, rsem):
    here = jnp.logical_and(dev[0] == me[0], dev[1] == me[1])
    remote = pltpu.make_async_remote_copy(
        src_ref=src, dst_ref=dst, send_sem=ssem, recv_sem=rsem, device_id=dev, device_id_type=MESH)

    @pl.when(here)
    def _():
        pltpu.make_async_copy(src, dst, rsem).start()

    @pl.when(jnp.logical_not(here))
    def _():
        remote.start()

    def drain():
        @pl.when(jnp.logical_not(here))
        def _():
            remote.wait_send()

    return drain


def gather_kernel(
    panels, a_hbm, v_ref, tri_ref,
    vth, vtl, yrows, zh, zl,
    a_mem, ah, al, vbuf, vh, vl, pbuf, cin, rin1, rin2, ytr, vcol, ycol, gpart, hpart, gmat, hmat, part,
    tin1, tin2, tin3, ct, dt,
    a_sem, vs, vr, ys, yr, vcs, vcr, ycs, ycr, gs, gr, hs, hr, cs, cr, zs, zr, ts, tr,
):
    pos = Place()
    me = pos.dev()
    nv, lanes = v_ref.shape
    nb = nv // panels
    rows, cols = a_mem.shape
    load = pltpu.make_async_copy(a_hbm, a_mem, a_sem)
    load.start()

    own_block = pos.y * 4 + pos.x
    vbuf[own_block] = v_ref[...]
    v_to, v_slot = pos.out_v()
    y_to, y_slot = pos.out_y()

    barrier = pltpu.get_barrier_semaphore()
    near = [pos.dev(x=wrap(pos.x, d)) for d in (1, 2, 3)]
    near += [pos.dev(y=wrap(pos.y, d)) for d in (1, 2, 3)]
    for d in range(1, 8):
        s = lax.rem(pos.s + d, 8)
        near.append(pos.dev(s // 2, lax.rem(s, 2)))
    near += [v_to, y_to]
    for dev in near:
        pl.semaphore_signal(barrier, inc=1, device_id=dev, device_id_type=MESH)
    pl.semaphore_wait(barrier, len(near))

    v_done = exchange(v_to, me, v_ref, vcol.at[v_slot], ts.at[0], tr.at[0])
    column_v = Column(pos, vcol, vcs, vcr)

    def column_start():
        own = vcol.at[pos.s]
        pltpu.make_async_copy(own, own, tr.at[0]).wait()
        column_v.start()

    gpart[...] = dotf(v_ref[...], v_ref[...], NT)
    total_g = Total(pos, gpart, gmat, part.at[0], tin1.at[0], tin2.at[0], tin3.at[0], gs, gr)

    ring_v = plane_gather(pos, vbuf, vs, vr, (total_g.step1, column_start))

    load.wait()

    @pl.loop(0, rows // lanes)
    def _(i):
        at = pl.ds(pl.multiple_of(i * lanes, lanes), lanes)
        ah[at], al[at] = split(a_mem[at])

    column_v.relay()
    total_g.step2()
    for b in range(16):
        high, low = split(vbuf[b])
        vh[:, b * lanes:(b + 1) * lanes] = high
        vl[:, b * lanes:(b + 1) * lanes] = low
    total_g.step3()
    column_v.finish()
    total_g.step4()

    @pl.loop(0, cols // (2 * lanes))
    def _(n):
        at = pl.ds(pl.multiple_of(n * 2 * lanes, 2 * lanes), 2 * lanes)
        value = dot3((vh[...], vl[...]), (ah[:, at], al[:, at]), NN)
        pbuf[n * 2] = value[:, :lanes]
        pbuf[n * 2 + 1] = value[:, lanes:]

    ring_c = Ring(cs, cr)
    partner = pos.dev(k=1 - pos.k)
    for q in range(4):
        ring_c.send(q, pbuf.at[2 * q + 1 - pos.k], cin.at[q], partner)

    acc = dotf(vcol[0], pbuf[0], NT)
    for s in range(1, 8):
        acc = acc + dotf(vcol[s], pbuf[s], NT)
    hpart[...] = acc
    total_h = Total(pos, hpart, hmat, part.at[1], tin1.at[1], tin2.at[1], tin3.at[1], hs, hr)
    total_h.step1()

    for q in range(4):
        ring_c.got(q, cin.at[q], me)
        mine = pbuf.at[2 * q + pos.k]
        cin[q] = cin[q] + mine[...]
    ring_z = Ring(zs, zr)
    half = nv // 2
    far, right, left = wrap(pos.z, 2), wrap(pos.z, 1), wrap(pos.z, -1)
    ring_z.send(0, cin.at[far, pl.ds(0, half)], rin1.at[0], pos.dev(z=right))
    ring_z.send(1, cin.at[far, pl.ds(half, half)], rin1.at[1], pos.dev(z=left))
    for n, to in ((0, right), (1, left)):
        ring_z.got(n, rin1.at[n], me)
        at = cin.at[to, pl.ds(n * half, half)]
        at[...] = at[...] + rin1[n]
        ring_z.send(2 + n, cin.at[to], rin2.at[n], pos.dev(z=to))
    total_h.step2()
    for n in (0, 1):
        ring_z.got(2 + n, rin2.at[n], me)
    shard = cin[pos.z] + rin2[0] + rin2[1]
    ycol[pos.s] = shard
    ytr[...] = shard.T
    y_done = exchange(y_to, me, ytr, yrows.at[y_slot], ts.at[1], tr.at[1])
    column_y = Column(pos, ycol, ycs, ycr)
    column_y.start()
    total_h.step3()
    pltpu.make_async_copy(ytr, yrows.at[own_block], tr.at[1]).wait()

    def middle():
        column_y.relay()
        total_h.step4()

    ring_y = plane_gather(pos, yrows, ys, yr, (middle,))
    column_y.finish()
    total_g.finish()
    total_h.finish()

    ct[...] = jnp.zeros_like(ct)
    dt[...] = jnp.zeros_like(dt)
    for p in range(panels):
        at = pl.ds(p * nb, nb)
        factor = split(tri_ref[p])
        pick = (lax.broadcasted_iota(jnp.int32, (nb, nv), 1)
                == lax.broadcasted_iota(jnp.int32, (nb, nv), 0) + p * nb).astype(F32)
        gp, hp = split(gmat[at]), split(hmat[at])
        c_all, d_all = split(ct[...]), split(dt[...])
        pc = pick - dot3(gp, c_all, NN)
        pd = -(dot3(hp, c_all, NT) + dot3(gp, d_all, NT) + dot3(gp, d_all, NN))
        ic, idt = dot3(factor, split(pc), TN), dot3(factor, split(pd), TN)
        inner = dot3(split(ic), hp, NT) + dot3(split(idt), gp, NT)
        coupling = dot3(split(inner), factor, NN)
        ct[at] = ic
        dt[at] = idt - 0.5 * dotf(coupling, pick, NN)
    c_pair = split(ct[...])
    ct_pair = split(ct[...].T)
    d_pair = split(dt[...] + dt[...].T)
    for s in range(8):
        at = slice(s * lanes, (s + 1) * lanes)
        vc, yc = split(vcol[s]), split(ycol[s])
        high, low = split(dot3(d_pair, vc, NN) + dot3(c_pair, yc, NN))
        zh[:nv, at], zl[:nv, at] = high, low
        high, low = split(dot3(ct_pair, vc, NN))
        zh[nv:, at], zl[nv:, at] = high, low

    @pl.loop(0, 16)
    def _(b):
        at = pl.ds(pl.multiple_of(b * lanes, lanes), lanes)
        vth[at], vtl[at] = split(vbuf[b].T)

    v_done()
    y_done()
    for ring in (ring_v, ring_c, ring_z, ring_y, column_v.ring, column_y.ring):
        ring.drain()


def update_kernel(a_ref, vth, vtl, y_ref, zh, zl, out_ref):
    nv = y_ref.shape[1]
    yh, yl = split(y_ref[...])
    z1 = (zh[:nv], zl[:nv])
    z2 = (zh[nv:], zl[nv:])
    out_ref[...] = a_ref[...] - (dot3((vth[...], vtl[...]), z1, NN) + dot3((yh, yl), z2, NN))


def shards(symmetric, reflectors, tri_factor):
    panels, nb, lanes = reflectors.shape
    nv = panels * nb
    rows, cols = symmetric.shape
    vmem = pl.BlockSpec(memory_space=pltpu.VMEM)
    dma = pltpu.SemaphoreType.DMA
    shape = jax.ShapeDtypeStruct
    vth, vtl, yrows, zh, zl = pl.pallas_call(
        functools.partial(gather_kernel, panels),
        out_shape=(
            shape((rows, nv), BF16), shape((rows, nv), BF16),
            shape((16, lanes, nv), F32),
            shape((2 * nv, cols), BF16), shape((2 * nv, cols), BF16),
        ),
        in_specs=[pl.BlockSpec(memory_space=pl.ANY), vmem, vmem],
        out_specs=(vmem,) * 5,
        scratch_shapes=[
            pltpu.VMEM((rows, cols), F32),
            pltpu.VMEM((rows, cols), BF16), pltpu.VMEM((rows, cols), BF16),
            pltpu.VMEM((16, nv, lanes), F32),
            pltpu.VMEM((nv, rows), BF16), pltpu.VMEM((nv, rows), BF16),
            pltpu.VMEM((8, nv, lanes), F32),
            pltpu.VMEM((4, nv, lanes), F32),
            pltpu.VMEM((2, nv // 2, lanes), F32),
            pltpu.VMEM((2, nv, lanes), F32),
            pltpu.VMEM((lanes, nv), F32),
            pltpu.VMEM((8, nv, lanes), F32), pltpu.VMEM((8, nv, lanes), F32),
            pltpu.VMEM((nv, nv), F32), pltpu.VMEM((nv, nv), F32),
            pltpu.VMEM((nv, nv), F32), pltpu.VMEM((nv, nv), F32),
            pltpu.VMEM((2, nv // 8, nv), F32),
            pltpu.VMEM((2, 7, nv // 8, nv), F32),
            pltpu.VMEM((2, 3, nv // 8, nv), F32),
            pltpu.VMEM((2, 4, nv // 8, nv), F32),
            pltpu.VMEM((nv, nv), F32), pltpu.VMEM((nv, nv), F32),
            dma, dma((40,)), dma((40,)), dma((40,)), dma((40,)),
            dma((8,)), dma((8,)), dma((8,)), dma((8,)),
            dma((20,)), dma((20,)), dma((20,)), dma((20,)),
            dma((4,)), dma((4,)), dma((4,)), dma((4,)), dma((2,)), dma((2,)),
        ],
        compiler_params=pltpu.CompilerParams(
            collective_id=0, has_side_effects=True, vmem_limit_bytes=56 * 2**20),
    )(symmetric, reflectors.reshape(nv, lanes), tri_factor)
    tile = 2 * lanes
    return pl.pallas_call(
        update_kernel,
        grid=(rows // tile,),
        out_shape=shape((rows, cols), F32),
        in_specs=[
            pl.BlockSpec((tile, cols), lambda i: (i, 0)),
            pl.BlockSpec((tile, nv), lambda i: (i, 0)),
            pl.BlockSpec((tile, nv), lambda i: (i, 0)),
            pl.BlockSpec((tile, nv), lambda i: (i, 0)),
            pl.BlockSpec((2 * nv, cols), lambda i: (0, 0)),
            pl.BlockSpec((2 * nv, cols), lambda i: (0, 0)),
        ],
        out_specs=pl.BlockSpec((tile, cols), lambda i: (i, 0)),
        compiler_params=pltpu.CompilerParams(vmem_limit_bytes=40 * 2**20),
    )(symmetric, vth, vtl, yrows.reshape(rows, nv), zh, zl)


def solution(mesh):
    placed = (P("row", "col"), P(None, None, ("row", "col")), P())
    return jax.shard_map(
        shards, mesh=mesh, in_specs=placed, out_specs=P("row", "col"), check_vma=False
    )
```

```python
import functools

import jax
import jax.numpy as jnp
from jax import lax
from jax.experimental import pallas as pl
from jax.experimental.pallas import tpu as pltpu
from jax.sharding import PartitionSpec as P

MESH = pl.DeviceIdType.MESH
F32 = jnp.float32
BF16 = jnp.bfloat16
NN = (((1,), (0,)), ((), ()))
NT = (((1,), (1,)), ((), ()))
TN = (((0,), (0,)), ((), ()))


def split(value):
    high = value.astype(BF16)
    return high, (value - high.astype(F32)).astype(BF16)


def dot3(left, right, dims):
    (lh, ll), (rh, rl) = left, right
    dot = functools.partial(lax.dot_general, dimension_numbers=dims, preferred_element_type=F32)
    return dot(lh, rh) + dot(lh, rl) + dot(ll, rh)


def dotf(left, right, dims):
    return dot3(split(left), split(right), dims)


class Place:
    def __init__(self):
        row, col = lax.axis_index("row"), lax.axis_index("col")
        self.z, self.k = row // 2, lax.rem(row, 2)
        self.y, self.x = col // 4, lax.rem(col, 4)
        self.s = row

    def dev(self, z=None, k=None, y=None, x=None):
        z = self.z if z is None else z
        k = self.k if k is None else k
        y = self.y if y is None else y
        x = self.x if x is None else x
        return (z * 2 + k, y * 4 + x)

    def out_v(self):
        s = lax.rem(self.y, 2) * 4 + self.x
        return self.dev(s // 2, lax.rem(s, 2), self.z, self.k * 2 + self.y // 2), s

    def out_y(self):
        side = 2 * lax.rem(self.x, 2) - 1
        x = lax.rem(self.x + side * self.k + 4, 4)
        y = lax.rem(self.y + self.z + 2 * self.k, 4)
        return self.dev(self.y, self.x // 2, y, x), y * 4 + x

    def from_v(self):
        b = lax.rem(self.x, 2) * 8 + self.s
        return self.dev(self.y, self.x // 2, b // 4, lax.rem(b, 4))

    def source(self, y, x):
        d = lax.rem(x - 2 * self.k + 4, 4)
        k = d // 2
        right = jnp.where(jnp.logical_or(d == 1, d == 2), 1, 0)
        z = lax.rem(y - self.z + 8 - 2 * k, 4)
        return right, z, k

    def from_y(self):
        right, z, k = self.source(self.y, self.x)
        return self.dev(z, k, self.z, 2 * self.k + right)

    def block_of(self, y, x):
        right, z, k = self.source(y, x)
        return right * 8 + 2 * z + k


def wrap(value, by):
    return lax.rem(value + by + 4, 4)


class Ring:
    def __init__(self, ssem, rsem):
        self.ssem, self.rsem = ssem, rsem
        self.sent = []

    def copy(self, i, src, dst, dev):
        return pltpu.make_async_remote_copy(
            src_ref=src, dst_ref=dst, send_sem=self.ssem.at[i], recv_sem=self.rsem.at[i],
            device_id=dev, device_id_type=MESH)

    def send(self, i, src, dst, dev):
        c = self.copy(i, src, dst, dev)
        c.start()
        self.sent.append(c)

    def got(self, i, ref, dev):
        self.copy(i, ref, ref, dev).wait_recv()

    def drain(self):
        for c in self.sent:
            c.wait_send()
        self.sent = []


def plane_gather(pos, buf, ssem, rsem, hooks=None):
    ring = Ring(ssem, rsem)
    rows = buf.shape[1]
    half, quarter = rows // 2, rows // 4
    me = pos.dev()

    class Half:
        def __init__(self, h):
            self.h, self.base = h, h * 20
            self.i, self.j = (pos.x, pos.y) if h == 0 else (pos.y, pos.x)

        def at(self, di, dj, part=None):
            i, j = wrap(self.i, di), wrap(self.j, dj)
            slot = j * 4 + i if self.h == 0 else i * 4 + j
            if part is None:
                return buf.at[slot, pl.ds(self.h * half, half)]
            return buf.at[slot, pl.ds(self.h * half + part * quarter, quarter)]

        def first(self, d):
            return pos.dev(x=wrap(pos.x, d)) if self.h == 0 else pos.dev(y=wrap(pos.y, d))

        def second(self, d):
            return pos.dev(y=wrap(pos.y, d)) if self.h == 0 else pos.dev(x=wrap(pos.x, d))

        def send1(self):
            for n, d in ((0, 1), (1, -1)):
                ring.send(self.base + n, self.at(0, 0), self.at(0, 0), self.first(d))

        def relay1(self, n):
            d = (-1, 1)[n]
            ring.got(self.base + n, self.at(d, 0), me)
            ref = self.at(d, 0, n)
            ring.send(self.base + 2 + n, ref, ref, self.first(-d))

        def far1(self):
            for n in (0, 1):
                ring.got(self.base + 2 + n, self.at(2, 0, n), me)

        def send2(self, c):
            di = (0, -1, 1, 2)[c]
            for n, d in ((0, 1), (1, -1)):
                ring.send(self.base + 4 + 4 * c + n, self.at(di, 0), self.at(di, 0), self.second(d))

        def relay2(self, c):
            di = (0, -1, 1, 2)[c]
            for n, d in ((0, -1), (1, 1)):
                ring.got(self.base + 4 + 4 * c + n, self.at(di, d), me)
                ref = self.at(di, d, n)
                ring.send(self.base + 4 + 4 * c + 2 + n, ref, ref, self.second(-d))

        def far2(self, c):
            di = (0, -1, 1, 2)[c]
            for n in (0, 1):
                ring.got(self.base + 4 + 4 * c + 2 + n, self.at(di, 2, n), me)

    hooks = hooks or {}
    hook = lambda n: [task() for task in hooks.get(n, ())]
    halves = (Half(0), Half(1))
    for h in halves:
        h.send1()
    for h in halves:
        h.send2(0)
    hook(0)
    for n in (0, 1):
        for h in halves:
            h.relay1(n)
            h.send2(1 + n)
    hook(1)
    for h in halves:
        h.relay2(0)
    hook(2)
    for h in halves:
        h.far1()
        h.send2(3)
    hook(3)
    for c in (1, 2, 3):
        for h in halves:
            h.relay2(c)
        hook(3 + c)
    for c in (0, 1, 2, 3):
        for h in halves:
            h.far2(c)
    return ring


class Column:
    def __init__(self, pos, buf, ssem, rsem):
        self.pos, self.buf = pos, buf
        self.ring = Ring(ssem, rsem)
        self.me = pos.dev()
        self.partner = pos.dev(k=1 - pos.k)
        self.quarter = buf.shape[1] // 2

    def at(self, dz, part=None, other=False):
        k = 1 - self.pos.k if other else self.pos.k
        slot = wrap(self.pos.z, dz) * 2 + k
        if part is None:
            return self.buf.at[slot]
        return self.buf.at[slot, pl.ds(part * self.quarter, self.quarter)]

    def zdev(self, d):
        return self.pos.dev(z=wrap(self.pos.z, d))

    def start(self):
        own = self.at(0)
        self.ring.send(0, own, own, self.zdev(1))
        self.ring.send(1, own, own, self.zdev(-1))
        self.ring.send(4, own, own, self.partner)

    def relay(self):
        for n, d in ((0, -1), (1, 1)):
            ref = self.at(d)
            self.ring.got(n, ref, self.me)
            part = self.at(d, n)
            self.ring.send(2 + n, part, part, self.zdev(-d))
            self.ring.send(5 + n, ref, ref, self.partner)

    def finish(self):
        for n in (0, 1):
            self.ring.got(2 + n, self.at(2, n), self.me)
        ref = self.at(2)
        self.ring.send(7, ref, ref, self.partner)
        for i, dz in ((4, 0), (5, -1), (6, 1), (7, 2)):
            self.ring.got(i, self.at(dz, other=True), self.me)


class Total:
    def __init__(self, pos, whole, out, part, in1, in2, in3, ssem, rsem):
        self.pos, self.whole, self.out, self.part = pos, whole, out, part
        self.ins = (in1, in2, in3)
        self.ring = Ring(ssem, rsem)
        self.me = pos.dev()
        self.rows = part.shape[0]

    def other(self, d):
        s = lax.rem(self.pos.s + d, 8)
        return s, self.pos.dev(s // 2, lax.rem(s, 2))

    def piece(self, s, ref=None):
        ref = self.whole if ref is None else ref
        return ref.at[pl.ds(pl.multiple_of(s * self.rows, self.rows), self.rows)]

    def step1(self):
        for d in range(1, 8):
            s, dev = self.other(d)
            self.ring.send(d - 1, self.piece(s), self.ins[0].at[d - 1], dev)

    def step2(self):
        value = self.piece(self.pos.s)[...]
        for d in range(7):
            self.ring.got(d, self.ins[0].at[d], self.me)
            value = value + self.ins[0][d]
        self.part[...] = value
        for d in (1, 2, 3):
            self.ring.send(6 + d, self.part, self.ins[1].at[d - 1], self.pos.dev(x=wrap(self.pos.x, d)))

    def step3(self):
        value = self.part[...]
        for d in (1, 2, 3):
            self.ring.got(6 + d, self.ins[1].at[d - 1], self.me)
            value = value + self.ins[1][d - 1]
        mid = self.ins[2].at[3]
        mid[...] = value
        for d in (1, 2, 3):
            self.ring.send(9 + d, mid, self.ins[2].at[d - 1], self.pos.dev(y=wrap(self.pos.y, d)))

    def step4(self):
        value = self.ins[2][3]
        for d in (1, 2, 3):
            self.ring.got(9 + d, self.ins[2].at[d - 1], self.me)
            value = value + self.ins[2][d - 1]
        own = self.piece(self.pos.s, self.out)
        own[...] = value
        for d in range(1, 8):
            _, dev = self.other(d)
            self.ring.send(12 + d, own, own, dev)

    def finish(self):
        for d in range(1, 8):
            s, _ = self.other(8 - d)
            self.ring.got(12 + d, self.piece(s, self.out), self.me)
        self.ring.drain()


def exchange(dev, me, src, dst, ssem, rsem):
    here = jnp.logical_and(dev[0] == me[0], dev[1] == me[1])
    remote = pltpu.make_async_remote_copy(
        src_ref=src, dst_ref=dst, send_sem=ssem, recv_sem=rsem, device_id=dev, device_id_type=MESH)

    @pl.when(here)
    def _():
        pltpu.make_async_copy(src, dst, rsem).start()

    @pl.when(jnp.logical_not(here))
    def _():
        remote.start()

    def drain():
        @pl.when(jnp.logical_not(here))
        def _():
            remote.wait_send()

    return drain


def panel_kernel(
    panels, a_hbm, v_ref, tri_ref, out_hbm,
    a_mem, ah, al, vbuf, vh, vl, pbuf, cin, rin1, rin2, ytr, colbuf, yrows,
    gpart, hpart, gmat, hmat, part, tin1, tin2, tin3, ct, dt, zh, zl,
    a_sem, o_sem, vs, vr, ys, yr, cols_s, cols_r, gs, gr, hs, hr, cs, cr, zs, zr, ts, tr,
):
    pos = Place()
    me = pos.dev()
    nv, lanes = v_ref.shape
    nb = nv // panels
    rows, cols = a_mem.shape
    load = pltpu.make_async_copy(a_hbm, a_mem, a_sem)
    load.start()

    vbuf[pos.y * 4 + pos.x] = v_ref[...]
    v_to, v_slot = pos.out_v()
    y_to, y_slot = pos.out_y()

    barrier = pltpu.get_barrier_semaphore()
    near = [pos.dev(x=wrap(pos.x, d)) for d in (1, 2, 3)]
    near += [pos.dev(y=wrap(pos.y, d)) for d in (1, 2, 3)]
    for d in range(1, 8):
        s = lax.rem(pos.s + d, 8)
        near.append(pos.dev(s // 2, lax.rem(s, 2)))
    near += [pos.from_v(), pos.from_y()]
    for dev in near:
        pl.semaphore_signal(barrier, inc=1, device_id=dev, device_id_type=MESH)
    pl.semaphore_wait(barrier, len(near))

    total_g = Total(pos, gpart, gmat, part.at[0], tin1.at[0], tin2.at[0], tin3.at[0], gs, gr)

    def gram():
        gpart[...] = dotf(v_ref[...], v_ref[...], NT)
        total_g.step1()

    def pairs():
        load.wait()

        @pl.loop(0, rows // lanes)
        def _(i):
            at = pl.ds(pl.multiple_of(i * lanes, lanes), lanes)
            ah[at], al[at] = split(a_mem[at])

    ring_v = plane_gather(pos, vbuf, vs, vr, {
        0: (gram,), 1: (pairs,), 3: (total_g.step2,), 5: (total_g.step3,)})
    v_done = exchange(v_to, me, v_ref, colbuf.at[v_slot, pl.ds(0, nv)], ts.at[0], tr.at[0])
    for b in range(16):
        high, low = split(vbuf[b])
        vh[:, b * lanes:(b + 1) * lanes] = high
        vl[:, b * lanes:(b + 1) * lanes] = low

    ring_c, ring_z = Ring(cs, cr), Ring(zs, zr)
    partner = pos.dev(k=1 - pos.k)
    half = nv // 2
    far, right, left = wrap(pos.z, 2), wrap(pos.z, 1), wrap(pos.z, -1)
    order = (far, right, left, pos.z)

    def product(i):
        at = pl.ds(pl.multiple_of(order[i] * 2 * lanes, 2 * lanes), 2 * lanes)
        value = dot3((vh[...], vl[...]), (ah[:, at], al[:, at]), NN)
        pbuf[2 * i] = value[:, :lanes]
        pbuf[2 * i + 1] = value[:, lanes:]
        ring_c.send(i, pbuf.at[2 * i + 1 - pos.k], cin.at[i], partner)

    def merge(i):
        ring_c.got(i, cin.at[i], me)
        cin[i] = cin[i] + pbuf[2 * i + pos.k]

    product(0)
    product(1)
    merge(0)
    ring_z.send(0, cin.at[0, pl.ds(0, half)], rin1.at[0], pos.dev(z=right))
    ring_z.send(1, cin.at[0, pl.ds(half, half)], rin1.at[1], pos.dev(z=left))
    product(2)
    product(3)
    total_g.step4()
    for n, to in ((0, right), (1, left)):
        merge(1 + n)
        ring_z.got(n, rin1.at[n], me)
        at = cin.at[1 + n, pl.ds(n * half, half)]
        at[...] = at[...] + rin1[n]
        ring_z.send(2 + n, cin.at[1 + n], rin2.at[n], pos.dev(z=to))
    merge(3)
    for n in (0, 1):
        ring_z.got(2 + n, rin2.at[n], me)
    shard = cin[3] + rin2[0] + rin2[1]
    ytr[...] = shard.T
    y_done = exchange(y_to, me, ytr, yrows.at[y_slot], ts.at[1], tr.at[1])
    colbuf[pos.s, nv:] = shard

    own_v = colbuf.at[pos.s, pl.ds(0, nv)]
    pltpu.make_async_copy(own_v, own_v, tr.at[0]).wait()
    hpart[...] = dotf(own_v[...], shard, NT)
    total_h = Total(pos, hpart, hmat, part.at[1], tin1.at[1], tin2.at[1], tin3.at[1], hs, hr)
    total_h.step1()
    column = Column(pos, colbuf, cols_s, cols_r)
    column.start()

    @pl.loop(0, 16)
    def _(b):
        at = pl.ds(pl.multiple_of(b * lanes, lanes), lanes)
        ah[at, :nv], al[at, :nv] = split(vbuf[b].T)

    total_h.step2()
    own_y = yrows.at[pos.y * 4 + pos.x]
    pltpu.make_async_copy(own_y, own_y, tr.at[1]).wait()

    ct[...] = jnp.zeros_like(ct)
    dt[...] = jnp.zeros_like(dt)

    def panel(p):
        at = pl.ds(p * nb, nb)
        factor = split(tri_ref[p])
        pick = (lax.broadcasted_iota(jnp.int32, (nb, nv), 1)
                == lax.broadcasted_iota(jnp.int32, (nb, nv), 0) + p * nb).astype(F32)
        gp, hp = split(gmat[at]), split(hmat[at])
        c_all, d_all = split(ct[...]), split(dt[...])
        pc = pick - dot3(gp, c_all, NN)
        pd = -(dot3(hp, c_all, NT) + dot3(gp, d_all, NT) + dot3(gp, d_all, NN))
        ic, idt = dot3(factor, split(pc), TN), dot3(factor, split(pd), TN)
        inner = dot3(split(ic), hp, NT) + dot3(split(idt), gp, NT)
        coupling = dot3(split(inner), factor, NN)
        ct[at] = ic
        dt[at] = idt - 0.5 * dotf(coupling, pick, NN)

    def first_panels():
        total_g.finish()
        total_h.finish()
        for p in range(panels // 2):
            panel(p)

    def last_panels():
        for p in range(panels // 2, panels):
            panel(p)

    def right_side():
        column.finish()
        c_pair = split(ct[...])
        ct_pair = split(ct[...].T)
        d_pair = split(dt[...] + dt[...].T)
        for s in range(8):
            at = slice(s * lanes, (s + 1) * lanes)
            vc, yc = split(colbuf[s, :nv]), split(colbuf[s, nv:])
            high, low = split(dot3(d_pair, vc, NN) + dot3(c_pair, yc, NN))
            zh[:nv, at], zl[:nv, at] = high, low
            high, low = split(dot3(ct_pair, vc, NN))
            zh[nv:, at], zl[nv:, at] = high, low

    tall, wide = 4 * lanes, 2 * lanes

    def reflector_part(lo, hi):
        @pl.loop(lo, hi)
        def _(g):
            at = pl.ds(pl.multiple_of(g * tall, tall), tall)
            left_pair = (ah[at, :nv], al[at, :nv])
            for n in range(cols // wide):
                to = slice(n * wide, (n + 1) * wide)
                a_mem[at, to] = a_mem[at, to] - dot3(left_pair, (zh[:nv, to], zl[:nv, to]), NN)

    ring_y = plane_gather(pos, yrows, ys, yr, {
        0: (total_h.step3, column.relay), 1: (total_h.step4,),
        3: (first_panels,), 4: (last_panels,), 5: (right_side,),
        6: (lambda: reflector_part(0, rows // tall),)})

    def written(b):
        at = pl.ds(pl.multiple_of(b * lanes, lanes), lanes)
        return pltpu.make_async_copy(a_mem.at[at], out_hbm.at[at], o_sem.at[b])

    @pl.loop(0, 4)
    def _(g):
        left_pair = split(yrows[pl.ds(g * 4, 4)].reshape(tall, nv))
        for n in range(cols // wide):
            to = slice(n * wide, (n + 1) * wide)
            value = dot3(left_pair, (zh[nv:, to], zl[nv:, to]), NN)
            for i in range(4):
                b = pos.block_of(g, i)
                at = pl.ds(pl.multiple_of(b * lanes, lanes), lanes)
                a_mem[at, to] = a_mem[at, to] - value[i * lanes:(i + 1) * lanes]
        for i in range(4):
            written(pos.block_of(g, i)).start()

    v_done()
    y_done()
    for ring in (ring_v, ring_c, ring_z, ring_y, column.ring):
        ring.drain()
    for b in range(16):
        written(b).wait()


def shards(symmetric, reflectors, tri_factor):
    panels, nb, lanes = reflectors.shape
    nv = panels * nb
    rows, cols = symmetric.shape
    vmem = pl.BlockSpec(memory_space=pltpu.VMEM)
    anywhere = pl.BlockSpec(memory_space=pl.ANY)
    dma = pltpu.SemaphoreType.DMA
    return pl.pallas_call(
        functools.partial(panel_kernel, panels),
        out_shape=jax.ShapeDtypeStruct((rows, cols), F32),
        in_specs=[anywhere, vmem, vmem],
        out_specs=anywhere,
        scratch_shapes=[
            pltpu.VMEM((rows, cols), F32),
            pltpu.VMEM((rows, cols), BF16), pltpu.VMEM((rows, cols), BF16),
            pltpu.VMEM((16, nv, lanes), F32),
            pltpu.VMEM((nv, rows), BF16), pltpu.VMEM((nv, rows), BF16),
            pltpu.VMEM((8, nv, lanes), F32),
            pltpu.VMEM((4, nv, lanes), F32),
            pltpu.VMEM((2, nv // 2, lanes), F32),
            pltpu.VMEM((2, nv, lanes), F32),
            pltpu.VMEM((lanes, nv), F32),
            pltpu.VMEM((8, 2 * nv, lanes), F32),
            pltpu.VMEM((16, lanes, nv), F32),
            pltpu.VMEM((nv, nv), F32), pltpu.VMEM((nv, nv), F32),
            pltpu.VMEM((nv, nv), F32), pltpu.VMEM((nv, nv), F32),
            pltpu.VMEM((2, nv // 8, nv), F32),
            pltpu.VMEM((2, 7, nv // 8, nv), F32),
            pltpu.VMEM((2, 3, nv // 8, nv), F32),
            pltpu.VMEM((2, 4, nv // 8, nv), F32),
            pltpu.VMEM((nv, nv), F32), pltpu.VMEM((nv, nv), F32),
            pltpu.VMEM((2 * nv, cols), BF16), pltpu.VMEM((2 * nv, cols), BF16),
            dma, dma((16,)), dma((40,)), dma((40,)), dma((40,)), dma((40,)),
            dma((8,)), dma((8,)),
            dma((20,)), dma((20,)), dma((20,)), dma((20,)),
            dma((4,)), dma((4,)), dma((4,)), dma((4,)), dma((2,)), dma((2,)),
        ],
        compiler_params=pltpu.CompilerParams(
            collective_id=0, has_side_effects=True, vmem_limit_bytes=56 * 2**20),
    )(symmetric, reflectors.reshape(nv, lanes), tri_factor)


def solution(mesh):
    placed = (P("row", "col"), P(None, None, ("row", "col")), P())
    return jax.shard_map(
        shards, mesh=mesh, in_specs=placed, out_specs=P("row", "col"), check_vma=False
    )
```

```python
import functools

import jax
import jax.numpy as jnp
from jax import lax
from jax.experimental import pallas as pl
from jax.experimental.pallas import tpu as pltpu
from jax.sharding import PartitionSpec as P

MESH = pl.DeviceIdType.MESH
F32 = jnp.float32
BF16 = jnp.bfloat16
NN = (((1,), (0,)), ((), ()))
NT = (((1,), (1,)), ((), ()))
TN = (((0,), (0,)), ((), ()))


def split(value):
    high = value.astype(BF16)
    return high, (value - high.astype(F32)).astype(BF16)


def dot3(left, right, dims):
    (lh, ll), (rh, rl) = left, right
    dot = functools.partial(lax.dot_general, dimension_numbers=dims, preferred_element_type=F32)
    return dot(lh, rh) + dot(lh, rl) + dot(ll, rh)


def dotf(left, right, dims):
    return dot3(split(left), split(right), dims)


class Place:
    def __init__(self):
        row, col = lax.axis_index("row"), lax.axis_index("col")
        self.z, self.k = row // 2, lax.rem(row, 2)
        self.y, self.x = col // 4, lax.rem(col, 4)
        self.s = row

    def dev(self, z=None, k=None, y=None, x=None):
        z = self.z if z is None else z
        k = self.k if k is None else k
        y = self.y if y is None else y
        x = self.x if x is None else x
        return (z * 2 + k, y * 4 + x)

    def out_v(self):
        s = lax.rem(self.y, 2) * 4 + self.x
        return self.dev(s // 2, lax.rem(s, 2), self.z, self.k * 2 + self.y // 2), s

    def out_y(self):
        side = 2 * lax.rem(self.x, 2) - 1
        x = lax.rem(self.x + side * self.k + 4, 4)
        y = lax.rem(self.y + self.z + 2 * self.k, 4)
        return self.dev(self.y, self.x // 2, y, x), y * 4 + x

    def from_v(self):
        b = lax.rem(self.x, 2) * 8 + self.s
        return self.dev(self.y, self.x // 2, b // 4, lax.rem(b, 4))

    def source(self, y, x):
        d = lax.rem(x - 2 * self.k + 4, 4)
        k = d // 2
        right = jnp.where(jnp.logical_or(d == 1, d == 2), 1, 0)
        z = lax.rem(y - self.z + 8 - 2 * k, 4)
        return right, z, k

    def from_y(self):
        right, z, k = self.source(self.y, self.x)
        return self.dev(z, k, self.z, 2 * self.k + right)

    def block_of(self, y, x):
        right, z, k = self.source(y, x)
        return right * 8 + 2 * z + k


def wrap(value, by):
    return lax.rem(value + by + 4, 4)


class Ring:
    def __init__(self, ssem, rsem):
        self.ssem, self.rsem = ssem, rsem
        self.sent = []

    def copy(self, i, src, dst, dev):
        return pltpu.make_async_remote_copy(
            src_ref=src, dst_ref=dst, send_sem=self.ssem.at[i], recv_sem=self.rsem.at[i],
            device_id=dev, device_id_type=MESH)

    def send(self, i, src, dst, dev):
        c = self.copy(i, src, dst, dev)
        c.start()
        self.sent.append(c)

    def got(self, i, ref, dev):
        self.copy(i, ref, ref, dev).wait_recv()

    def drain(self):
        for c in self.sent:
            c.wait_send()
        self.sent = []


def plane_gather(pos, buf, ssem, rsem, hooks=None):
    ring = Ring(ssem, rsem)
    rows = buf.shape[1]
    half, quarter = rows // 2, rows // 4
    me = pos.dev()

    class Half:
        def __init__(self, h):
            self.h, self.base = h, h * 20
            self.i, self.j = (pos.x, pos.y) if h == 0 else (pos.y, pos.x)

        def at(self, di, dj, part=None):
            i, j = wrap(self.i, di), wrap(self.j, dj)
            slot = j * 4 + i if self.h == 0 else i * 4 + j
            if part is None:
                return buf.at[slot, pl.ds(self.h * half, half)]
            return buf.at[slot, pl.ds(self.h * half + part * quarter, quarter)]

        def first(self, d):
            return pos.dev(x=wrap(pos.x, d)) if self.h == 0 else pos.dev(y=wrap(pos.y, d))

        def second(self, d):
            return pos.dev(y=wrap(pos.y, d)) if self.h == 0 else pos.dev(x=wrap(pos.x, d))

        def send1(self):
            for n, d in ((0, 1), (1, -1)):
                ring.send(self.base + n, self.at(0, 0), self.at(0, 0), self.first(d))

        def relay1(self, n):
            d = (-1, 1)[n]
            ring.got(self.base + n, self.at(d, 0), me)
            ref = self.at(d, 0, n)
            ring.send(self.base + 2 + n, ref, ref, self.first(-d))

        def far1(self):
            for n in (0, 1):
                ring.got(self.base + 2 + n, self.at(2, 0, n), me)

        def send2(self, c):
            di = (0, -1, 1, 2)[c]
            for n, d in ((0, 1), (1, -1)):
                ring.send(self.base + 4 + 4 * c + n, self.at(di, 0), self.at(di, 0), self.second(d))

        def relay2(self, c):
            di = (0, -1, 1, 2)[c]
            for n, d in ((0, -1), (1, 1)):
                ring.got(self.base + 4 + 4 * c + n, self.at(di, d), me)
                ref = self.at(di, d, n)
                ring.send(self.base + 4 + 4 * c + 2 + n, ref, ref, self.second(-d))

        def far2(self, c):
            di = (0, -1, 1, 2)[c]
            for n in (0, 1):
                ring.got(self.base + 4 + 4 * c + 2 + n, self.at(di, 2, n), me)

    hooks = hooks or {}
    hook = lambda n: [task() for task in hooks.get(n, ())]
    halves = (Half(0), Half(1))
    for h in halves:
        h.send1()
    for h in halves:
        h.send2(0)
    hook(0)
    for n in (0, 1):
        for h in halves:
            h.relay1(n)
            h.send2(1 + n)
    hook(1)
    for h in halves:
        h.relay2(0)
    hook(2)
    for h in halves:
        h.far1()
        h.send2(3)
    hook(3)
    for c in (1, 2, 3):
        for h in halves:
            h.relay2(c)
        hook(3 + c)
    for c in (0, 1, 2, 3):
        for h in halves:
            h.far2(c)
    return ring


class Column:
    def __init__(self, pos, buf, ssem, rsem):
        self.pos, self.buf = pos, buf
        self.ring = Ring(ssem, rsem)
        self.me = pos.dev()
        self.partner = pos.dev(k=1 - pos.k)
        self.quarter = buf.shape[1] // 2

    def at(self, dz, part=None, other=False):
        k = 1 - self.pos.k if other else self.pos.k
        slot = wrap(self.pos.z, dz) * 2 + k
        if part is None:
            return self.buf.at[slot]
        return self.buf.at[slot, pl.ds(part * self.quarter, self.quarter)]

    def zdev(self, d):
        return self.pos.dev(z=wrap(self.pos.z, d))

    def start(self):
        own = self.at(0)
        self.ring.send(0, own, own, self.zdev(1))
        self.ring.send(1, own, own, self.zdev(-1))
        self.ring.send(4, own, own, self.partner)

    def relay(self):
        for n, d in ((0, -1), (1, 1)):
            ref = self.at(d)
            self.ring.got(n, ref, self.me)
            part = self.at(d, n)
            self.ring.send(2 + n, part, part, self.zdev(-d))
            self.ring.send(5 + n, ref, ref, self.partner)

    def finish(self):
        for n in (0, 1):
            self.ring.got(2 + n, self.at(2, n), self.me)
        ref = self.at(2)
        self.ring.send(7, ref, ref, self.partner)
        for i, dz in ((4, 0), (5, -1), (6, 1), (7, 2)):
            self.ring.got(i, self.at(dz, other=True), self.me)


class Total:
    def __init__(self, pos, whole, out, part, in1, in2, in3, ssem, rsem):
        self.pos, self.whole, self.out, self.part = pos, whole, out, part
        self.ins = (in1, in2, in3)
        self.ring = Ring(ssem, rsem)
        self.me = pos.dev()

    def other(self, d):
        s = lax.rem(self.pos.s + d, 8)
        return s, self.pos.dev(s // 2, lax.rem(s, 2))

    def piece(self, s, ref=None):
        ref = self.whole if ref is None else ref
        return ref.at[s]

    def step1(self):
        for d in range(1, 8):
            s, dev = self.other(d)
            self.ring.send(d - 1, self.piece(s), self.ins[0].at[d - 1], dev)

    def step2(self):
        value = self.piece(self.pos.s)[...]
        for d in range(7):
            self.ring.got(d, self.ins[0].at[d], self.me)
            value = value + self.ins[0][d]
        self.part[...] = value
        for d in (1, 2, 3):
            self.ring.send(6 + d, self.part, self.ins[1].at[d - 1], self.pos.dev(x=wrap(self.pos.x, d)))

    def step3(self):
        value = self.part[...]
        for d in (1, 2, 3):
            self.ring.got(6 + d, self.ins[1].at[d - 1], self.me)
            value = value + self.ins[1][d - 1]
        mid = self.ins[2].at[3]
        mid[...] = value
        for d in (1, 2, 3):
            self.ring.send(9 + d, mid, self.ins[2].at[d - 1], self.pos.dev(y=wrap(self.pos.y, d)))

    def step4(self):
        value = self.ins[2][3]
        for d in (1, 2, 3):
            self.ring.got(9 + d, self.ins[2].at[d - 1], self.me)
            value = value + self.ins[2][d - 1]
        own = self.piece(self.pos.s, self.out)
        own[...] = value
        for d in range(1, 8):
            _, dev = self.other(d)
            self.ring.send(12 + d, own, own, dev)

    def finish(self):
        for d in range(1, 8):
            s, _ = self.other(8 - d)
            self.ring.got(12 + d, self.piece(s, self.out), self.me)
        self.ring.drain()


def exchange(dev, me, src, dst, ssem, rsem):
    here = jnp.logical_and(dev[0] == me[0], dev[1] == me[1])
    remote = pltpu.make_async_remote_copy(
        src_ref=src, dst_ref=dst, send_sem=ssem, recv_sem=rsem, device_id=dev, device_id_type=MESH)

    @pl.when(here)
    def _():
        pltpu.make_async_copy(src, dst, rsem).start()

    @pl.when(jnp.logical_not(here))
    def _():
        remote.start()

    def drain():
        @pl.when(jnp.logical_not(here))
        def _():
            remote.wait_send()

    return drain


def panel_kernel(
    panels, a_hbm, v_ref, tri_ref, mid_hbm, y_hbm, zh_hbm, zl_hbm,
    a_mem, ah, al, vbuf, vh, vl, pbuf, cin, rin1, rin2, ytr, colbuf, yrows,
    packed, summed, gmat, hmat, part, tin1, tin2, tin3, ct, dt, zh, zl, yzh, yzl,
    a_sem, m_sem, o_sem, z_sem, vs, vr, ys, yr, cols_s, cols_r, hs, hr, cs, cr, zs, zr, ts, tr,
):
    pos = Place()
    me = pos.dev()
    nv, lanes = v_ref.shape
    nb = nv // panels
    rows, cols = a_mem.shape
    load = pltpu.make_async_copy(a_hbm, a_mem, a_sem)
    load.start()

    vbuf[pos.y * 4 + pos.x] = v_ref[...]
    v_to, v_slot = pos.out_v()
    y_to, y_slot = pos.out_y()

    barrier = pltpu.get_barrier_semaphore()
    near = [pos.dev(x=wrap(pos.x, d)) for d in (1, 2, 3)]
    near += [pos.dev(y=wrap(pos.y, d)) for d in (1, 2, 3)]
    for d in range(1, 8):
        s = lax.rem(pos.s + d, 8)
        near.append(pos.dev(s // 2, lax.rem(s, 2)))
    near += [pos.from_v(), pos.from_y()]
    for dev in near:
        pl.semaphore_signal(barrier, inc=1, device_id=dev, device_id_type=MESH)
    pl.semaphore_wait(barrier, len(near))

    def pairs():
        load.wait()

        @pl.loop(0, rows // lanes)
        def _(i):
            at = pl.ds(pl.multiple_of(i * lanes, lanes), lanes)
            ah[at], al[at] = split(a_mem[at])

    ring_v = plane_gather(pos, vbuf, vs, vr, {1: (pairs,)})
    v_done = exchange(v_to, me, v_ref, colbuf.at[v_slot, pl.ds(0, nv)], ts.at[0], tr.at[0])
    for b in range(16):
        high, low = split(vbuf[b])
        vh[:, b * lanes:(b + 1) * lanes] = high
        vl[:, b * lanes:(b + 1) * lanes] = low

    ring_c, ring_z = Ring(cs, cr), Ring(zs, zr)
    partner = pos.dev(k=1 - pos.k)
    half = nv // 2
    far, right, left = wrap(pos.z, 2), wrap(pos.z, 1), wrap(pos.z, -1)
    order = (far, right, left, pos.z)

    def product(i):
        at = pl.ds(pl.multiple_of(order[i] * 2 * lanes, 2 * lanes), 2 * lanes)
        value = dot3((vh[...], vl[...]), (ah[:, at], al[:, at]), NN)
        pbuf[2 * i] = value[:, :lanes]
        pbuf[2 * i + 1] = value[:, lanes:]
        ring_c.send(i, pbuf.at[2 * i + 1 - pos.k], cin.at[i], partner)

    def merge(i):
        ring_c.got(i, cin.at[i], me)
        cin[i] = cin[i] + pbuf[2 * i + pos.k]

    product(0)
    product(1)
    merge(0)
    ring_z.send(0, cin.at[0, pl.ds(0, half)], rin1.at[0], pos.dev(z=right))
    ring_z.send(1, cin.at[0, pl.ds(half, half)], rin1.at[1], pos.dev(z=left))
    product(2)
    product(3)
    for n, to in ((0, right), (1, left)):
        merge(1 + n)
        ring_z.got(n, rin1.at[n], me)
        at = cin.at[1 + n, pl.ds(n * half, half)]
        at[...] = at[...] + rin1[n]
        ring_z.send(2 + n, cin.at[1 + n], rin2.at[n], pos.dev(z=to))
    merge(3)
    for n in (0, 1):
        ring_z.got(2 + n, rin2.at[n], me)
    shard = cin[3] + rin2[0] + rin2[1]
    ytr[...] = shard.T
    y_done = exchange(y_to, me, ytr, yrows.at[y_slot], ts.at[1], tr.at[1])
    colbuf[pos.s, nv:] = shard

    own_v = colbuf.at[pos.s, pl.ds(0, nv)]
    pltpu.make_async_copy(own_v, own_v, tr.at[0]).wait()
    row = lax.broadcasted_iota(jnp.int32, (nv, nv), 0)
    column_index = lax.broadcasted_iota(jnp.int32, (nv, nv), 1)
    below, on = row >= column_index, row == column_index
    group = nv // 8
    gram = dotf(v_ref[...], v_ref[...], NT)
    packed[:, group:] = jnp.zeros_like(packed[:, group:])
    packed[:, :group] = jnp.where(below, dotf(own_v[...], shard, NT), gram).reshape(8, group, nv)
    packed[0, group:group + 1] = jnp.sum(jnp.where(on, gram, 0.0), axis=0, keepdims=True)
    total = Total(pos, packed, summed, part, tin1, tin2, tin3, hs, hr)
    total.step1()
    column = Column(pos, colbuf, cols_s, cols_r)
    column.start()

    @pl.loop(0, 16)
    def _(b):
        at = pl.ds(pl.multiple_of(b * lanes, lanes), lanes)
        ah[at, :nv], al[at, :nv] = split(vbuf[b].T)

    total.step2()
    own_y = yrows.at[pos.y * 4 + pos.x]
    pltpu.make_async_copy(own_y, own_y, tr.at[1]).wait()

    ct[...] = jnp.zeros_like(ct)
    dt[...] = jnp.zeros_like(dt)

    def panel(p):
        at = pl.ds(p * nb, nb)
        factor = split(tri_ref[p])
        pick = (lax.broadcasted_iota(jnp.int32, (nb, nv), 1)
                == lax.broadcasted_iota(jnp.int32, (nb, nv), 0) + p * nb).astype(F32)
        gp, hp = split(gmat[at]), split(hmat[at])
        c_all, d_all = split(ct[...]), split(dt[...])
        pc = pick - dot3(gp, c_all, NN)
        pd = -(dot3(hp, c_all, NT) + dot3(gp, d_all, NT) + dot3(gp, d_all, NN))
        ic, idt = dot3(factor, split(pc), TN), dot3(factor, split(pd), TN)
        inner = dot3(split(ic), hp, NT) + dot3(split(idt), gp, NT)
        coupling = dot3(split(inner), factor, NN)
        ct[at] = ic
        dt[at] = idt - 0.5 * dotf(coupling, pick, NN)

    def inner_products():
        total.finish()
        both = summed[:, :group].reshape(nv, nv)
        turned = both.T
        hmat[...] = jnp.where(below, both, turned)
        gmat[...] = jnp.where(on, summed[0, group:group + 1], jnp.where(below, turned, both))

    def coefficients():
        for p in range(panels):
            panel(p)

    right_copies = (
        pltpu.make_async_copy(yzh, zh_hbm, z_sem.at[0]), pltpu.make_async_copy(yzl, zl_hbm, z_sem.at[1]))

    def right_side():
        c_pair = split(ct[...])
        ct_pair = split(ct[...].T)
        d_pair = split(dt[...] + dt[...].T)
        for s in range(8):
            at = slice(s * lanes, (s + 1) * lanes)
            vc, yc = split(colbuf[s, :nv]), split(colbuf[s, nv:])
            zh[:, at], zl[:, at] = split(dot3(d_pair, vc, NN) + dot3(c_pair, yc, NN))
            yzh[:, at], yzl[:, at] = split(dot3(ct_pair, vc, NN))
        for copy in right_copies:
            copy.start()

    tall, wide = 4 * lanes, 2 * lanes

    def middle_copy(g):
        at = pl.ds(pl.multiple_of(g * tall, tall), tall)
        return pltpu.make_async_copy(a_mem.at[at], mid_hbm.at[at], m_sem.at[g])

    def reflector_part():
        @pl.loop(0, rows // tall)
        def _(g):
            at = pl.ds(pl.multiple_of(g * tall, tall), tall)
            left_pair = (ah[at, :nv], al[at, :nv])
            for n in range(cols // wide):
                to = slice(n * wide, (n + 1) * wide)
                a_mem[at, to] = a_mem[at, to] - dot3(left_pair, (zh[:, to], zl[:, to]), NN)
            middle_copy(g).start()

    ring_y = plane_gather(pos, yrows, ys, yr, {
        0: (total.step3, column.relay), 2: (total.step4,),
        6: (column.finish, inner_products, coefficients, right_side, reflector_part)})

    def row_copy(slot):
        b = pos.block_of(slot // 4, slot % 4)
        return pltpu.make_async_copy(yrows.at[slot], y_hbm.at[b], o_sem.at[slot])

    for slot in range(16):
        row_copy(slot).start()
    v_done()
    y_done()
    for ring in (ring_v, ring_c, ring_z, ring_y, column.ring):
        ring.drain()
    for copy in right_copies:
        copy.wait()
    for g in range(rows // tall):
        middle_copy(g).wait()
    for slot in range(16):
        row_copy(slot).wait()


def product_kernel(mid_ref, y_ref, zh, zl, out_ref):
    out_ref[...] = mid_ref[...] - dot3(split(y_ref[...]), (zh[...], zl[...]), NN)


def shards(symmetric, reflectors, tri_factor):
    panels, nb, lanes = reflectors.shape
    nv = panels * nb
    rows, cols = symmetric.shape
    vmem = pl.BlockSpec(memory_space=pltpu.VMEM)
    anywhere = pl.BlockSpec(memory_space=pl.ANY)
    dma = pltpu.SemaphoreType.DMA
    shape = jax.ShapeDtypeStruct
    middle, y_rows, zh, zl = pl.pallas_call(
        functools.partial(panel_kernel, panels),
        out_shape=(
            shape((rows, cols), F32), shape((16, lanes, nv), F32),
            shape((nv, cols), BF16), shape((nv, cols), BF16)),
        in_specs=[anywhere, vmem, vmem],
        out_specs=(anywhere,) * 4,
        scratch_shapes=[
            pltpu.VMEM((rows, cols), F32),
            pltpu.VMEM((rows, cols), BF16), pltpu.VMEM((rows, cols), BF16),
            pltpu.VMEM((16, nv, lanes), F32),
            pltpu.VMEM((nv, rows), BF16), pltpu.VMEM((nv, rows), BF16),
            pltpu.VMEM((8, nv, lanes), F32),
            pltpu.VMEM((4, nv, lanes), F32),
            pltpu.VMEM((2, nv // 2, lanes), F32),
            pltpu.VMEM((2, nv, lanes), F32),
            pltpu.VMEM((lanes, nv), F32),
            pltpu.VMEM((8, 2 * nv, lanes), F32),
            pltpu.VMEM((16, lanes, nv), F32),
            pltpu.VMEM((8, nv // 8 + 8, nv), F32), pltpu.VMEM((8, nv // 8 + 8, nv), F32),
            pltpu.VMEM((nv, nv), F32), pltpu.VMEM((nv, nv), F32),
            pltpu.VMEM((nv // 8 + 8, nv), F32),
            pltpu.VMEM((7, nv // 8 + 8, nv), F32),
            pltpu.VMEM((3, nv // 8 + 8, nv), F32),
            pltpu.VMEM((4, nv // 8 + 8, nv), F32),
            pltpu.VMEM((nv, nv), F32), pltpu.VMEM((nv, nv), F32),
            pltpu.VMEM((nv, cols), BF16), pltpu.VMEM((nv, cols), BF16),
            pltpu.VMEM((nv, cols), BF16), pltpu.VMEM((nv, cols), BF16),
            dma, dma((4,)), dma((16,)), dma((2,)),
            dma((40,)), dma((40,)), dma((40,)), dma((40,)),
            dma((8,)), dma((8,)), dma((20,)), dma((20,)),
            dma((4,)), dma((4,)), dma((4,)), dma((4,)), dma((2,)), dma((2,)),
        ],
        compiler_params=pltpu.CompilerParams(
            collective_id=0, has_side_effects=True, vmem_limit_bytes=56 * 2**20),
    )(symmetric, reflectors.reshape(nv, lanes), tri_factor)
    tile = 2 * lanes
    return pl.pallas_call(
        product_kernel,
        grid=(rows // tile,),
        out_shape=shape((rows, cols), F32),
        in_specs=[
            pl.BlockSpec((tile, cols), lambda i: (i, 0)),
            pl.BlockSpec((tile, nv), lambda i: (i, 0)),
            pl.BlockSpec((nv, cols), lambda i: (0, 0)),
            pl.BlockSpec((nv, cols), lambda i: (0, 0)),
        ],
        out_specs=pl.BlockSpec((tile, cols), lambda i: (i, 0)),
        compiler_params=pltpu.CompilerParams(vmem_limit_bytes=58 * 2**20),
    )(middle, y_rows.reshape(rows, nv), zh, zl)


def solution(mesh):
    placed = (P("row", "col"), P(None, None, ("row", "col")), P())
    return jax.shard_map(
        shards, mesh=mesh, in_specs=placed, out_specs=P("row", "col"), check_vma=False
    )
```

```python
import functools

import jax
import jax.numpy as jnp
from jax import lax
from jax.experimental import pallas as pl
from jax.experimental.pallas import tpu as pltpu
from jax.sharding import PartitionSpec as P

MESH = pl.DeviceIdType.MESH
F32 = jnp.float32
BF16 = jnp.bfloat16
NN = (((1,), (0,)), ((), ()))
NT = (((1,), (1,)), ((), ()))
TN = (((0,), (0,)), ((), ()))


def split(value):
    high = value.astype(BF16)
    return high, (value - high.astype(F32)).astype(BF16)


def dot3(left, right, dims):
    (lh, ll), (rh, rl) = left, right
    dot = functools.partial(lax.dot_general, dimension_numbers=dims, preferred_element_type=F32)
    return dot(lh, rh) + dot(lh, rl) + dot(ll, rh)


def dotf(left, right, dims):
    return dot3(split(left), split(right), dims)


class Place:
    def __init__(self):
        row, col = lax.axis_index("row"), lax.axis_index("col")
        self.z, self.k = row // 2, lax.rem(row, 2)
        self.y, self.x = col // 4, lax.rem(col, 4)
        self.s = row

    def dev(self, z=None, k=None, y=None, x=None):
        z = self.z if z is None else z
        k = self.k if k is None else k
        y = self.y if y is None else y
        x = self.x if x is None else x
        return (z * 2 + k, y * 4 + x)

    def out_v(self):
        s = lax.rem(self.y, 2) * 4 + self.x
        return self.dev(s // 2, lax.rem(s, 2), self.z, self.k * 2 + self.y // 2), s

    def out_y(self):
        side = 2 * lax.rem(self.x, 2) - 1
        x = lax.rem(self.x + side * self.k + 4, 4)
        y = lax.rem(self.y + self.z + 2 * self.k, 4)
        return self.dev(self.y, self.x // 2, y, x), y * 4 + x

    def from_v(self):
        b = lax.rem(self.x, 2) * 8 + self.s
        return self.dev(self.y, self.x // 2, b // 4, lax.rem(b, 4))

    def source(self, y, x):
        d = lax.rem(x - 2 * self.k + 4, 4)
        k = d // 2
        right = jnp.where(jnp.logical_or(d == 1, d == 2), 1, 0)
        z = lax.rem(y - self.z + 8 - 2 * k, 4)
        return right, z, k

    def from_y(self):
        right, z, k = self.source(self.y, self.x)
        return self.dev(z, k, self.z, 2 * self.k + right)

    def block_of(self, y, x):
        right, z, k = self.source(y, x)
        return right * 8 + 2 * z + k


def wrap(value, by):
    return lax.rem(value + by + 4, 4)


class Ring:
    def __init__(self, ssem, rsem):
        self.ssem, self.rsem = ssem, rsem
        self.sent = []

    def copy(self, i, src, dst, dev):
        return pltpu.make_async_remote_copy(
            src_ref=src, dst_ref=dst, send_sem=self.ssem.at[i], recv_sem=self.rsem.at[i],
            device_id=dev, device_id_type=MESH)

    def send(self, i, src, dst, dev):
        c = self.copy(i, src, dst, dev)
        c.start()
        self.sent.append(c)

    def got(self, i, ref, dev):
        self.copy(i, ref, ref, dev).wait_recv()

    def drain(self):
        for c in self.sent:
            c.wait_send()
        self.sent = []


def plane_gather(pos, buf, ssem, rsem, hooks=None):
    ring = Ring(ssem, rsem)
    rows = buf.shape[1]
    half, quarter = rows // 2, rows // 4
    me = pos.dev()
    direct = (3,)

    class Half:
        def __init__(self, h):
            self.h, self.base = h, h * 20
            self.i, self.j = (pos.x, pos.y) if h == 0 else (pos.y, pos.x)

        def at(self, di, dj, part=None):
            i, j = wrap(self.i, di), wrap(self.j, dj)
            slot = j * 4 + i if self.h == 0 else i * 4 + j
            if part is None:
                return buf.at[slot, pl.ds(self.h * half, half)]
            return buf.at[slot, pl.ds(self.h * half + part * quarter, quarter)]

        def first(self, d):
            return pos.dev(x=wrap(pos.x, d)) if self.h == 0 else pos.dev(y=wrap(pos.y, d))

        def second(self, d):
            return pos.dev(y=wrap(pos.y, d)) if self.h == 0 else pos.dev(x=wrap(pos.x, d))

        def send1(self):
            for n, d in ((0, 1), (1, -1)):
                ring.send(self.base + n, self.at(0, 0), self.at(0, 0), self.first(d))
            ring.send(self.base + 2, self.at(0, 0), self.at(0, 0), self.first(2))

        def relay1(self, n):
            d = (-1, 1)[n]
            ring.got(self.base + n, self.at(d, 0), me)

        def far1(self):
            ring.got(self.base + 2, self.at(2, 0), me)

        def send2(self, c):
            di = (0, -1, 1, 2)[c]
            for n, d in ((0, 1), (1, -1)):
                ring.send(self.base + 4 + 4 * c + n, self.at(di, 0), self.at(di, 0), self.second(d))
            if c in direct:
                ring.send(self.base + 6 + 4 * c, self.at(di, 0), self.at(di, 0), self.second(2))

        def relay2(self, c):
            di = (0, -1, 1, 2)[c]
            for n, d in ((0, -1), (1, 1)):
                ring.got(self.base + 4 + 4 * c + n, self.at(di, d), me)
                if c not in direct:
                    ref = self.at(di, d, n)
                    ring.send(self.base + 6 + 4 * c + n, ref, ref, self.second(-d))

        def far2(self, c):
            di = (0, -1, 1, 2)[c]
            if c in direct:
                return ring.got(self.base + 6 + 4 * c, self.at(di, 2), me)
            for n in (0, 1):
                ring.got(self.base + 6 + 4 * c + n, self.at(di, 2, n), me)

    hooks = hooks or {}
    hook = lambda n: [task() for task in hooks.get(n, ())]
    halves = (Half(0), Half(1))
    for h in halves:
        h.send1()
    for h in halves:
        h.send2(0)
    hook(0)
    for n in (0, 1):
        for h in halves:
            h.relay1(n)
            h.send2(1 + n)
    hook(1)
    for h in halves:
        h.relay2(0)
    hook(2)
    for h in halves:
        h.far1()
        h.send2(3)
    hook(3)
    for c in (1, 2, 3):
        for h in halves:
            h.relay2(c)
        hook(3 + c)
    for c in (0, 1, 2, 3):
        for h in halves:
            h.far2(c)
    return ring


class Column:
    def __init__(self, pos, buf, ssem, rsem):
        self.pos, self.buf = pos, buf
        self.ring = Ring(ssem, rsem)
        self.me = pos.dev()
        self.partner = pos.dev(k=1 - pos.k)
        self.quarter = buf.shape[1] // 2

    def at(self, dz, part=None, other=False):
        k = 1 - self.pos.k if other else self.pos.k
        slot = wrap(self.pos.z, dz) * 2 + k
        if part is None:
            return self.buf.at[slot]
        return self.buf.at[slot, pl.ds(part * self.quarter, self.quarter)]

    def zdev(self, d):
        return self.pos.dev(z=wrap(self.pos.z, d))

    def start(self):
        own = self.at(0)
        self.ring.send(0, own, own, self.zdev(1))
        self.ring.send(1, own, own, self.zdev(-1))
        self.ring.send(4, own, own, self.partner)

    def relay(self):
        for n, d in ((0, -1), (1, 1)):
            ref = self.at(d)
            self.ring.got(n, ref, self.me)
            part = self.at(d, n)
            self.ring.send(2 + n, part, part, self.zdev(-d))
            self.ring.send(5 + n, ref, ref, self.partner)

    def finish(self):
        for n in (0, 1):
            self.ring.got(2 + n, self.at(2, n), self.me)
        ref = self.at(2)
        self.ring.send(7, ref, ref, self.partner)
        for i, dz in ((4, 0), (5, -1), (6, 1), (7, 2)):
            self.ring.got(i, self.at(dz, other=True), self.me)


class Total:
    def __init__(self, pos, whole, out, part, in1, in2, in3, ssem, rsem):
        self.pos, self.whole, self.out, self.part = pos, whole, out, part
        self.ins = (in1, in2, in3)
        self.ring = Ring(ssem, rsem)
        self.me = pos.dev()

    def other(self, d):
        s = lax.rem(self.pos.s + d, 8)
        return s, self.pos.dev(s // 2, lax.rem(s, 2))

    def piece(self, s, ref=None):
        ref = self.whole if ref is None else ref
        return ref.at[s]

    def step1(self):
        for d in range(1, 8):
            s, dev = self.other(d)
            self.ring.send(d - 1, self.piece(s), self.ins[0].at[d - 1], dev)

    def step2(self):
        value = self.piece(self.pos.s)[...]
        for d in range(7):
            self.ring.got(d, self.ins[0].at[d], self.me)
            value = value + self.ins[0][d]
        self.part[...] = value
        for d in (1, 2, 3):
            self.ring.send(6 + d, self.part, self.ins[1].at[d - 1], self.pos.dev(x=wrap(self.pos.x, d)))

    def step3(self):
        value = self.part[...]
        for d in (1, 2, 3):
            self.ring.got(6 + d, self.ins[1].at[d - 1], self.me)
            value = value + self.ins[1][d - 1]
        mid = self.ins[2].at[3]
        mid[...] = value
        for d in (1, 2, 3):
            self.ring.send(9 + d, mid, self.ins[2].at[d - 1], self.pos.dev(y=wrap(self.pos.y, d)))

    def step4(self):
        value = self.ins[2][3]
        for d in (1, 2, 3):
            self.ring.got(9 + d, self.ins[2].at[d - 1], self.me)
            value = value + self.ins[2][d - 1]
        own = self.piece(self.pos.s, self.out)
        own[...] = value
        for d in range(1, 8):
            _, dev = self.other(d)
            self.ring.send(12 + d, own, own, dev)

    def finish(self):
        for d in range(1, 8):
            s, _ = self.other(8 - d)
            self.ring.got(12 + d, self.piece(s, self.out), self.me)
        self.ring.drain()


def exchange(dev, me, src, dst, ssem, rsem):
    here = jnp.logical_and(dev[0] == me[0], dev[1] == me[1])
    remote = pltpu.make_async_remote_copy(
        src_ref=src, dst_ref=dst, send_sem=ssem, recv_sem=rsem, device_id=dev, device_id_type=MESH)

    @pl.when(here)
    def _():
        pltpu.make_async_copy(src, dst, rsem).start()

    @pl.when(jnp.logical_not(here))
    def _():
        remote.start()

    def drain():
        @pl.when(jnp.logical_not(here))
        def _():
            remote.wait_send()

    return drain


def panel_kernel(
    panels, a_hbm, v_hbm, tri_hbm, mid_hbm, y_hbm, zh_hbm, zl_hbm,
    a_mem, ah, al, vbuf, vh, vl, pbuf, cin, rin1, rin2, ytr, colbuf, yrows,
    packed, summed, gmat, hmat, part, tin1, tin2, tin3, ct, dt, zh, zl, yzh, yzl, tri_ref,
    a_sem, in_sem, m_sem, o_sem, z_sem, vs, vr, ys, yr, cols_s, cols_r, hs, hr, cs, cr, zs, zr, ts, tr,
):
    pos = Place()
    me = pos.dev()
    own = pos.y * 4 + pos.x
    v_ref = vbuf.at[own]
    nv, lanes = v_ref.shape
    nb = nv // panels
    rows, cols = a_mem.shape
    small = (
        pltpu.make_async_copy(v_hbm, v_ref, in_sem.at[0]), pltpu.make_async_copy(tri_hbm, tri_ref, in_sem.at[1]))
    for copy in small:
        copy.start()
    load = pltpu.make_async_copy(a_hbm, a_mem, a_sem)
    load.start()

    v_to, v_slot = pos.out_v()
    y_to, y_slot = pos.out_y()

    barrier = pltpu.get_barrier_semaphore()
    near = [pos.dev(x=wrap(pos.x, d)) for d in (1, 2, 3)]
    near += [pos.dev(y=wrap(pos.y, d)) for d in (1, 2, 3)]
    for d in range(1, 8):
        s = lax.rem(pos.s + d, 8)
        near.append(pos.dev(s // 2, lax.rem(s, 2)))
    near += [pos.from_v(), pos.from_y()]
    for dev in near:
        pl.semaphore_signal(barrier, inc=1, device_id=dev, device_id_type=MESH)
    for copy in small:
        copy.wait()
    pl.semaphore_wait(barrier, len(near))

    def pairs():
        load.wait()

        @pl.loop(0, rows // lanes)
        def _(i):
            at = pl.ds(pl.multiple_of(i * lanes, lanes), lanes)
            ah[at], al[at] = split(a_mem[at])

    ring_v = plane_gather(pos, vbuf, vs, vr, {1: (pairs,)})
    v_done = exchange(v_to, me, v_ref, colbuf.at[v_slot, pl.ds(0, nv)], ts.at[0], tr.at[0])
    for b in range(16):
        high, low = split(vbuf[b])
        vh[:, b * lanes:(b + 1) * lanes] = high
        vl[:, b * lanes:(b + 1) * lanes] = low

    ring_c, ring_z = Ring(cs, cr), Ring(zs, zr)
    partner = pos.dev(k=1 - pos.k)
    half = nv // 2
    far, right, left = wrap(pos.z, 2), wrap(pos.z, 1), wrap(pos.z, -1)
    order = (far, right, left, pos.z)

    def product(i):
        at = pl.ds(pl.multiple_of(order[i] * 2 * lanes, 2 * lanes), 2 * lanes)
        value = dot3((vh[...], vl[...]), (ah[:, at], al[:, at]), NN)
        pbuf[2 * i] = value[:, :lanes]
        pbuf[2 * i + 1] = value[:, lanes:]
        ring_c.send(i, pbuf.at[2 * i + 1 - pos.k], cin.at[i], partner)

    def merge(i):
        ring_c.got(i, cin.at[i], me)
        cin[i] = cin[i] + pbuf[2 * i + pos.k]

    product(0)
    product(1)
    merge(0)
    ring_z.send(0, cin.at[0, pl.ds(0, half)], rin1.at[0], pos.dev(z=right))
    ring_z.send(1, cin.at[0, pl.ds(half, half)], rin1.at[1], pos.dev(z=left))
    product(2)
    product(3)
    for n, to in ((0, right), (1, left)):
        merge(1 + n)
        ring_z.got(n, rin1.at[n], me)
        at = cin.at[1 + n, pl.ds(n * half, half)]
        at[...] = at[...] + rin1[n]
        ring_z.send(2 + n, cin.at[1 + n], rin2.at[n], pos.dev(z=to))
    merge(3)
    for n in (0, 1):
        ring_z.got(2 + n, rin2.at[n], me)
    shard = cin[3] + rin2[0] + rin2[1]
    ytr[...] = shard.T
    y_done = exchange(y_to, me, ytr, yrows.at[y_slot], ts.at[1], tr.at[1])
    colbuf[pos.s, nv:] = shard

    own_v = colbuf.at[pos.s, pl.ds(0, nv)]
    pltpu.make_async_copy(own_v, own_v, tr.at[0]).wait()
    row = lax.broadcasted_iota(jnp.int32, (nv, nv), 0)
    column_index = lax.broadcasted_iota(jnp.int32, (nv, nv), 1)
    below, on = row >= column_index, row == column_index
    group = nv // 8
    gram = dotf(v_ref[...], v_ref[...], NT)
    packed[:, group:] = jnp.zeros_like(packed[:, group:])
    packed[:, :group] = jnp.where(below, dotf(own_v[...], shard, NT), gram).reshape(8, group, nv)
    packed[0, group:group + 1] = jnp.sum(jnp.where(on, gram, 0.0), axis=0, keepdims=True)
    total = Total(pos, packed, summed, part, tin1, tin2, tin3, hs, hr)
    total.step1()
    column = Column(pos, colbuf, cols_s, cols_r)
    column.start()

    @pl.loop(0, 16)
    def _(b):
        at = pl.ds(pl.multiple_of(b * lanes, lanes), lanes)
        ah[at, :nv], al[at, :nv] = split(vbuf[b].T)

    total.step2()
    own_y = yrows.at[pos.y * 4 + pos.x]
    pltpu.make_async_copy(own_y, own_y, tr.at[1]).wait()

    ct[...] = jnp.zeros_like(ct)
    dt[...] = jnp.zeros_like(dt)

    def panel(p):
        at = pl.ds(p * nb, nb)
        factor = split(tri_ref[p])
        pick = (lax.broadcasted_iota(jnp.int32, (nb, nv), 1)
                == lax.broadcasted_iota(jnp.int32, (nb, nv), 0) + p * nb).astype(F32)
        gp, hp = split(gmat[at]), split(hmat[at])
        c_all, d_all = split(ct[...]), split(dt[...])
        pc = pick - dot3(gp, c_all, NN)
        pd = -(dot3(hp, c_all, NT) + dot3(gp, d_all, NT) + dot3(gp, d_all, NN))
        ic, idt = dot3(factor, split(pc), TN), dot3(factor, split(pd), TN)
        inner = dot3(split(ic), hp, NT) + dot3(split(idt), gp, NT)
        coupling = dot3(split(inner), factor, NN)
        ct[at] = ic
        dt[at] = idt - 0.5 * dotf(coupling, pick, NN)

    def inner_products():
        total.finish()
        both = summed[:, :group].reshape(nv, nv)
        turned = both.T
        hmat[...] = jnp.where(below, both, turned)
        gmat[...] = jnp.where(on, summed[0, group:group + 1], jnp.where(below, turned, both))

    def coefficients():
        for p in range(panels):
            panel(p)

    right_copies = (
        pltpu.make_async_copy(yzh, zh_hbm, z_sem.at[0]), pltpu.make_async_copy(yzl, zl_hbm, z_sem.at[1]))

    def right_side():
        c_pair = split(ct[...])
        ct_pair = split(ct[...].T)
        d_pair = split(dt[...] + dt[...].T)
        for s in range(8):
            at = slice(s * lanes, (s + 1) * lanes)
            vc, yc = split(colbuf[s, :nv]), split(colbuf[s, nv:])
            zh[:, at], zl[:, at] = split(dot3(d_pair, vc, NN) + dot3(c_pair, yc, NN))
            yzh[:, at], yzl[:, at] = split(dot3(ct_pair, vc, NN))
        for copy in right_copies:
            copy.start()

    tall, wide = 4 * lanes, 2 * lanes

    def middle_copy(g):
        at = pl.ds(pl.multiple_of(g * tall, tall), tall)
        return pltpu.make_async_copy(a_mem.at[at], mid_hbm.at[at], m_sem.at[g])

    def reflector_part():
        @pl.loop(0, rows // tall)
        def _(g):
            at = pl.ds(pl.multiple_of(g * tall, tall), tall)
            left_pair = (ah[at, :nv], al[at, :nv])
            for n in range(cols // wide):
                to = slice(n * wide, (n + 1) * wide)
                a_mem[at, to] = a_mem[at, to] - dot3(left_pair, (zh[:, to], zl[:, to]), NN)
            middle_copy(g).start()

    ring_y = plane_gather(pos, yrows, ys, yr, {
        0: (total.step3, column.relay), 2: (total.step4,),
        6: (column.finish, inner_products, coefficients, right_side, reflector_part)})

    def row_copy(slot):
        b = pos.block_of(slot // 4, slot % 4)
        return pltpu.make_async_copy(yrows.at[slot], y_hbm.at[b], o_sem.at[slot])

    for slot in range(16):
        row_copy(slot).start()
    v_done()
    y_done()
    for ring in (ring_v, ring_c, ring_z, ring_y, column.ring):
        ring.drain()
    for copy in right_copies:
        copy.wait()
    for g in range(rows // tall):
        middle_copy(g).wait()
    for slot in range(16):
        row_copy(slot).wait()


def product_kernel(mid_ref, y_ref, zh, zl, out_ref):
    out_ref[...] = mid_ref[...] - dot3(split(y_ref[...]), (zh[...], zl[...]), NN)


def shards(symmetric, reflectors, tri_factor):
    panels, nb, lanes = reflectors.shape
    nv = panels * nb
    rows, cols = symmetric.shape
    anywhere = pl.BlockSpec(memory_space=pl.ANY)
    dma = pltpu.SemaphoreType.DMA
    shape = jax.ShapeDtypeStruct
    middle, y_rows, zh, zl = pl.pallas_call(
        functools.partial(panel_kernel, panels),
        out_shape=(
            shape((rows, cols), F32), shape((16, lanes, nv), F32),
            shape((nv, cols), BF16), shape((nv, cols), BF16)),
        in_specs=[pl.BlockSpec(memory_space=pltpu.HBM)] * 3,
        out_specs=(anywhere,) * 4,
        scratch_shapes=[
            pltpu.VMEM((rows, cols), F32),
            pltpu.VMEM((rows, cols), BF16), pltpu.VMEM((rows, cols), BF16),
            pltpu.VMEM((16, nv, lanes), F32),
            pltpu.VMEM((nv, rows), BF16), pltpu.VMEM((nv, rows), BF16),
            pltpu.VMEM((8, nv, lanes), F32),
            pltpu.VMEM((4, nv, lanes), F32),
            pltpu.VMEM((2, nv // 2, lanes), F32),
            pltpu.VMEM((2, nv, lanes), F32),
            pltpu.VMEM((lanes, nv), F32),
            pltpu.VMEM((8, 2 * nv, lanes), F32),
            pltpu.VMEM((16, lanes, nv), F32),
            pltpu.VMEM((8, nv // 8 + 8, nv), F32), pltpu.VMEM((8, nv // 8 + 8, nv), F32),
            pltpu.VMEM((nv, nv), F32), pltpu.VMEM((nv, nv), F32),
            pltpu.VMEM((nv // 8 + 8, nv), F32),
            pltpu.VMEM((7, nv // 8 + 8, nv), F32),
            pltpu.VMEM((3, nv // 8 + 8, nv), F32),
            pltpu.VMEM((4, nv // 8 + 8, nv), F32),
            pltpu.VMEM((nv, nv), F32), pltpu.VMEM((nv, nv), F32),
            pltpu.VMEM((nv, cols), BF16), pltpu.VMEM((nv, cols), BF16),
            pltpu.VMEM((nv, cols), BF16), pltpu.VMEM((nv, cols), BF16),
            pltpu.VMEM(tri_factor.shape, F32),
            dma, dma((2,)), dma((4,)), dma((16,)), dma((2,)),
            dma((40,)), dma((40,)), dma((40,)), dma((40,)),
            dma((8,)), dma((8,)), dma((20,)), dma((20,)),
            dma((4,)), dma((4,)), dma((4,)), dma((4,)), dma((2,)), dma((2,)),
        ],
        compiler_params=pltpu.CompilerParams(
            collective_id=0, has_side_effects=True, vmem_limit_bytes=34 * 2**20),
    )(*(pltpu.with_memory_space_constraint(v, pltpu.HBM) for v in (symmetric, reflectors.reshape(nv, lanes), tri_factor)))
    tile = 2 * lanes
    return pl.pallas_call(
        product_kernel,
        grid=(rows // tile,),
        out_shape=shape((rows, cols), F32),
        in_specs=[
            pl.BlockSpec((tile, cols), lambda i: (i, 0)),
            pl.BlockSpec((tile, nv), lambda i: (i, 0)),
            pl.BlockSpec((nv, cols), lambda i: (0, 0)),
            pl.BlockSpec((nv, cols), lambda i: (0, 0)),
        ],
        out_specs=pl.BlockSpec((tile, cols), lambda i: (i, 0)),
        compiler_params=pltpu.CompilerParams(vmem_limit_bytes=16 * 2**20),
    )(middle, y_rows.reshape(rows, nv), zh, zl)


def solution(mesh):
    placed = (P("row", "col"), P(None, None, ("row", "col")), P())
    return jax.shard_map(
        shards, mesh=mesh, in_specs=placed, out_specs=P("row", "col"), check_vma=False
    )
```

```python
import functools

import jax
import jax.numpy as jnp
from jax import lax
from jax.experimental import pallas as pl
from jax.experimental.pallas import tpu as pltpu
from jax.sharding import PartitionSpec as P

MESH = pl.DeviceIdType.MESH
F32 = jnp.float32
BF16 = jnp.bfloat16
NN = (((1,), (0,)), ((), ()))
NT = (((1,), (1,)), ((), ()))
TN = (((0,), (0,)), ((), ()))


def split(value):
    high = value.astype(BF16)
    return high, (value - high.astype(F32)).astype(BF16)


def dot3(left, right, dims):
    (lh, ll), (rh, rl) = left, right
    dot = functools.partial(lax.dot_general, dimension_numbers=dims, preferred_element_type=F32)
    return dot(lh, rh) + dot(lh, rl) + dot(ll, rh)


def dotf(left, right, dims):
    return dot3(split(left), split(right), dims)


class Place:
    def __init__(self):
        row, col = lax.axis_index("row"), lax.axis_index("col")
        self.z, self.k = row // 2, lax.rem(row, 2)
        self.y, self.x = col // 4, lax.rem(col, 4)
        self.s = row

    def dev(self, z=None, k=None, y=None, x=None):
        z = self.z if z is None else z
        k = self.k if k is None else k
        y = self.y if y is None else y
        x = self.x if x is None else x
        return (z * 2 + k, y * 4 + x)

    def out_v(self):
        s = lax.rem(self.y, 2) * 4 + self.x
        return self.dev(s // 2, lax.rem(s, 2), self.z, self.k * 2 + self.y // 2), s

    def out_y(self):
        side = 2 * lax.rem(self.x, 2) - 1
        x = lax.rem(self.x + side * self.k + 4, 4)
        y = lax.rem(self.y + self.z + 2 * self.k, 4)
        return self.dev(self.y, self.x // 2, y, x), y * 4 + x

    def from_v(self):
        b = lax.rem(self.x, 2) * 8 + self.s
        return self.dev(self.y, self.x // 2, b // 4, lax.rem(b, 4))

    def source(self, y, x):
        d = lax.rem(x - 2 * self.k + 4, 4)
        k = d // 2
        right = jnp.where(jnp.logical_or(d == 1, d == 2), 1, 0)
        z = lax.rem(y - self.z + 8 - 2 * k, 4)
        return right, z, k

    def from_y(self):
        right, z, k = self.source(self.y, self.x)
        return self.dev(z, k, self.z, 2 * self.k + right)

    def block_of(self, y, x):
        right, z, k = self.source(y, x)
        return right * 8 + 2 * z + k


def wrap(value, by):
    return lax.rem(value + by + 4, 4)


class Ring:
    def __init__(self, ssem, rsem):
        self.ssem, self.rsem = ssem, rsem
        self.sent = []

    def copy(self, i, src, dst, dev):
        return pltpu.make_async_remote_copy(
            src_ref=src, dst_ref=dst, send_sem=self.ssem.at[i], recv_sem=self.rsem.at[i],
            device_id=dev, device_id_type=MESH)

    def send(self, i, src, dst, dev):
        c = self.copy(i, src, dst, dev)
        c.start()
        self.sent.append(c)

    def got(self, i, ref, dev):
        self.copy(i, ref, ref, dev).wait_recv()

    def drain(self):
        for c in self.sent:
            c.wait_send()
        self.sent = []


def plane_gather(pos, buf, ssem, rsem, hooks=None):
    ring = Ring(ssem, rsem)
    rows = buf.shape[1]
    half, quarter = rows // 2, rows // 4
    me = pos.dev()
    direct = (3,)

    class Half:
        def __init__(self, h):
            self.h, self.base = h, h * 20
            self.i, self.j = (pos.x, pos.y) if h == 0 else (pos.y, pos.x)

        def at(self, di, dj, part=None):
            i, j = wrap(self.i, di), wrap(self.j, dj)
            slot = j * 4 + i if self.h == 0 else i * 4 + j
            if part is None:
                return buf.at[slot, pl.ds(self.h * half, half)]
            return buf.at[slot, pl.ds(self.h * half + part * quarter, quarter)]

        def first(self, d):
            return pos.dev(x=wrap(pos.x, d)) if self.h == 0 else pos.dev(y=wrap(pos.y, d))

        def second(self, d):
            return pos.dev(y=wrap(pos.y, d)) if self.h == 0 else pos.dev(x=wrap(pos.x, d))

        def send1(self):
            for n, d in ((0, 1), (1, -1)):
                ring.send(self.base + n, self.at(0, 0), self.at(0, 0), self.first(d))
            ring.send(self.base + 2, self.at(0, 0), self.at(0, 0), self.first(2))

        def relay1(self, n):
            d = (-1, 1)[n]
            ring.got(self.base + n, self.at(d, 0), me)

        def far1(self):
            ring.got(self.base + 2, self.at(2, 0), me)

        def send2(self, c):
            di = (0, -1, 1, 2)[c]
            for n, d in ((0, 1), (1, -1)):
                ring.send(self.base + 4 + 4 * c + n, self.at(di, 0), self.at(di, 0), self.second(d))
            if c in direct:
                ring.send(self.base + 6 + 4 * c, self.at(di, 0), self.at(di, 0), self.second(2))

        def relay2(self, c):
            di = (0, -1, 1, 2)[c]
            for n, d in ((0, -1), (1, 1)):
                ring.got(self.base + 4 + 4 * c + n, self.at(di, d), me)
                if c not in direct:
                    ref = self.at(di, d, n)
                    ring.send(self.base + 6 + 4 * c + n, ref, ref, self.second(-d))

        def far2(self, c):
            di = (0, -1, 1, 2)[c]
            if c in direct:
                return ring.got(self.base + 6 + 4 * c, self.at(di, 2), me)
            for n in (0, 1):
                ring.got(self.base + 6 + 4 * c + n, self.at(di, 2, n), me)

    hooks = hooks or {}
    hook = lambda n: [task() for task in hooks.get(n, ())]
    halves = (Half(0), Half(1))
    for h in halves:
        h.send1()
    for h in halves:
        h.send2(0)
    hook(0)
    for n in (0, 1):
        for h in halves:
            h.relay1(n)
            h.send2(1 + n)
    hook(1)
    for h in halves:
        h.far1()
        h.send2(3)
    hook(2)
    for h in halves:
        h.relay2(0)
    hook(3)
    for c in (1, 2, 3):
        for h in halves:
            h.relay2(c)
        hook(3 + c)
    for c in (0, 1, 2, 3):
        for h in halves:
            h.far2(c)
    return ring


class Column:
    def __init__(self, pos, buf, ssem, rsem):
        self.pos, self.buf = pos, buf
        self.ring = Ring(ssem, rsem)
        self.me = pos.dev()
        self.partner = pos.dev(k=1 - pos.k)
        self.quarter = buf.shape[1] // 2

    def at(self, dz, part=None, other=False):
        k = 1 - self.pos.k if other else self.pos.k
        slot = wrap(self.pos.z, dz) * 2 + k
        if part is None:
            return self.buf.at[slot]
        return self.buf.at[slot, pl.ds(part * self.quarter, self.quarter)]

    def zdev(self, d):
        return self.pos.dev(z=wrap(self.pos.z, d))

    def start(self):
        own = self.at(0)
        self.ring.send(0, own, own, self.zdev(1))
        self.ring.send(1, own, own, self.zdev(-1))
        self.ring.send(4, own, own, self.partner)

    def relay(self):
        for n, d in ((0, -1), (1, 1)):
            ref = self.at(d)
            self.ring.got(n, ref, self.me)
            part = self.at(d, n)
            self.ring.send(2 + n, part, part, self.zdev(-d))
            self.ring.send(5 + n, ref, ref, self.partner)

    def finish(self):
        for n in (0, 1):
            self.ring.got(2 + n, self.at(2, n), self.me)
        ref = self.at(2)
        self.ring.send(7, ref, ref, self.partner)
        for i, dz in ((4, 0), (5, -1), (6, 1), (7, 2)):
            self.ring.got(i, self.at(dz, other=True), self.me)


class Total:
    def __init__(self, pos, whole, out, part, in1, in2, in3, ssem, rsem):
        self.pos, self.whole, self.out, self.part = pos, whole, out, part
        self.ins = (in1, in2, in3)
        self.ring = Ring(ssem, rsem)
        self.me = pos.dev()

    def other(self, d):
        s = lax.rem(self.pos.s + d, 8)
        return s, self.pos.dev(s // 2, lax.rem(s, 2))

    def piece(self, s, ref=None):
        ref = self.whole if ref is None else ref
        return ref.at[s]

    def step1(self):
        for d in range(1, 8):
            s, dev = self.other(d)
            self.ring.send(d - 1, self.piece(s), self.ins[0].at[d - 1], dev)

    def step2(self):
        value = self.piece(self.pos.s)[...]
        for d in range(7):
            self.ring.got(d, self.ins[0].at[d], self.me)
            value = value + self.ins[0][d]
        self.part[...] = value
        for d in (1, 2, 3):
            self.ring.send(6 + d, self.part, self.ins[1].at[d - 1], self.pos.dev(x=wrap(self.pos.x, d)))

    def step3(self):
        value = self.part[...]
        for d in (1, 2, 3):
            self.ring.got(6 + d, self.ins[1].at[d - 1], self.me)
            value = value + self.ins[1][d - 1]
        mid = self.ins[2].at[3]
        mid[...] = value
        for d in (1, 2, 3):
            self.ring.send(9 + d, mid, self.ins[2].at[d - 1], self.pos.dev(y=wrap(self.pos.y, d)))

    def step4(self):
        value = self.ins[2][3]
        for d in (1, 2, 3):
            self.ring.got(9 + d, self.ins[2].at[d - 1], self.me)
            value = value + self.ins[2][d - 1]
        own = self.piece(self.pos.s, self.out)
        own[...] = value
        for d in range(1, 8):
            _, dev = self.other(d)
            self.ring.send(12 + d, own, own, dev)

    def finish(self):
        for d in range(1, 8):
            s, _ = self.other(8 - d)
            self.ring.got(12 + d, self.piece(s, self.out), self.me)
        self.ring.drain()


def exchange(dev, me, src, dst, ssem, rsem):
    here = jnp.logical_and(dev[0] == me[0], dev[1] == me[1])
    remote = pltpu.make_async_remote_copy(
        src_ref=src, dst_ref=dst, send_sem=ssem, recv_sem=rsem, device_id=dev, device_id_type=MESH)

    @pl.when(here)
    def _():
        pltpu.make_async_copy(src, dst, rsem).start()

    @pl.when(jnp.logical_not(here))
    def _():
        remote.start()

    def drain():
        @pl.when(jnp.logical_not(here))
        def _():
            remote.wait_send()

    return drain


def panel_kernel(
    panels, a_hbm, v_hbm, tri_hbm, mid_hbm, y_hbm, zh_hbm, zl_hbm,
    a_mem, ah, al, vbuf, vh, vl, pbuf, cin, rin1, rin2, ytr, colbuf, yrows,
    packed, summed, gmat, hmat, part, tin1, tin2, tin3, ct, dt, zh, zl, yzh, yzl, tri_ref,
    a_sem, in_sem, m_sem, o_sem, z_sem, vs, vr, ys, yr, cols_s, cols_r, hs, hr, cs, cr, zs, zr, ts, tr,
):
    pos = Place()
    me = pos.dev()
    own = pos.y * 4 + pos.x
    v_ref = vbuf.at[own]
    nv, lanes = v_ref.shape
    nb = nv // panels
    rows, cols = a_mem.shape
    small = (
        pltpu.make_async_copy(v_hbm, v_ref, in_sem.at[0]), pltpu.make_async_copy(tri_hbm, tri_ref, in_sem.at[1]))
    for copy in small:
        copy.start()
    load = pltpu.make_async_copy(a_hbm, a_mem, a_sem)
    load.start()

    v_to, v_slot = pos.out_v()
    y_to, y_slot = pos.out_y()

    barrier = pltpu.get_barrier_semaphore()
    near = [pos.dev(x=wrap(pos.x, d)) for d in (1, 2, 3)]
    near += [pos.dev(y=wrap(pos.y, d)) for d in (1, 2, 3)]
    for d in range(1, 8):
        s = lax.rem(pos.s + d, 8)
        near.append(pos.dev(s // 2, lax.rem(s, 2)))
    near += [pos.from_v(), pos.from_y()]
    for dev in near:
        pl.semaphore_signal(barrier, inc=1, device_id=dev, device_id_type=MESH)
    for copy in small:
        copy.wait()
    pl.semaphore_wait(barrier, len(near))

    def pairs():
        load.wait()

        @pl.loop(0, rows // lanes)
        def _(i):
            at = pl.ds(pl.multiple_of(i * lanes, lanes), lanes)
            ah[at], al[at] = split(a_mem[at])

    ring_v = plane_gather(pos, vbuf, vs, vr, {6: (pairs,)})
    v_done = exchange(v_to, me, v_ref, colbuf.at[v_slot, pl.ds(0, nv)], ts.at[0], tr.at[0])
    for b in range(16):
        high, low = split(vbuf[b])
        vh[:, b * lanes:(b + 1) * lanes] = high
        vl[:, b * lanes:(b + 1) * lanes] = low

    ring_c, ring_z = Ring(cs, cr), Ring(zs, zr)
    partner = pos.dev(k=1 - pos.k)
    half = nv // 2
    far, right, left = wrap(pos.z, 2), wrap(pos.z, 1), wrap(pos.z, -1)
    order = (far, right, left, pos.z)

    def product(i):
        at = pl.ds(pl.multiple_of(order[i] * 2 * lanes, 2 * lanes), 2 * lanes)
        value = dot3((vh[...], vl[...]), (ah[:, at], al[:, at]), NN)
        pbuf[2 * i] = value[:, :lanes]
        pbuf[2 * i + 1] = value[:, lanes:]
        ring_c.send(i, pbuf.at[2 * i + 1 - pos.k], cin.at[i], partner)

    def merge(i):
        ring_c.got(i, cin.at[i], me)
        cin[i] = cin[i] + pbuf[2 * i + pos.k]

    product(0)
    product(1)
    merge(0)
    ring_z.send(0, cin.at[0, pl.ds(0, half)], rin1.at[0], pos.dev(z=right))
    ring_z.send(1, cin.at[0, pl.ds(half, half)], rin1.at[1], pos.dev(z=left))
    product(2)
    product(3)
    for n, to in ((0, right), (1, left)):
        merge(1 + n)
        ring_z.got(n, rin1.at[n], me)
        at = cin.at[1 + n, pl.ds(n * half, half)]
        at[...] = at[...] + rin1[n]
        ring_z.send(2 + n, cin.at[1 + n], rin2.at[n], pos.dev(z=to))
    merge(3)
    for n in (0, 1):
        ring_z.got(2 + n, rin2.at[n], me)
    shard = cin[3] + rin2[0] + rin2[1]
    ytr[...] = shard.T
    y_done = exchange(y_to, me, ytr, yrows.at[y_slot], ts.at[1], tr.at[1])
    colbuf[pos.s, nv:] = shard

    own_v = colbuf.at[pos.s, pl.ds(0, nv)]
    pltpu.make_async_copy(own_v, own_v, tr.at[0]).wait()
    row = lax.broadcasted_iota(jnp.int32, (nv, nv), 0)
    column_index = lax.broadcasted_iota(jnp.int32, (nv, nv), 1)
    below, on = row >= column_index, row == column_index
    group = nv // 8
    gram = dotf(v_ref[...], v_ref[...], NT)
    packed[:, group:] = jnp.zeros_like(packed[:, group:])
    packed[:, :group] = jnp.where(below, dotf(own_v[...], shard, NT), gram).reshape(8, group, nv)
    packed[0, group:group + 1] = jnp.sum(jnp.where(on, gram, 0.0), axis=0, keepdims=True)
    total = Total(pos, packed, summed, part, tin1, tin2, tin3, hs, hr)
    total.step1()
    column = Column(pos, colbuf, cols_s, cols_r)
    column.start()

    @pl.loop(0, 16)
    def _(b):
        at = pl.ds(pl.multiple_of(b * lanes, lanes), lanes)
        ah[at, :nv], al[at, :nv] = split(vbuf[b].T)

    total.step2()
    own_y = yrows.at[pos.y * 4 + pos.x]
    pltpu.make_async_copy(own_y, own_y, tr.at[1]).wait()

    ct[...] = jnp.zeros_like(ct)
    dt[...] = jnp.zeros_like(dt)

    def panel(p):
        at = pl.ds(p * nb, nb)
        factor = split(tri_ref[p])
        pick = (lax.broadcasted_iota(jnp.int32, (nb, nv), 1)
                == lax.broadcasted_iota(jnp.int32, (nb, nv), 0) + p * nb).astype(F32)
        gp, hp = split(gmat[at]), split(hmat[at])
        c_all, d_all = split(ct[...]), split(dt[...])
        pc = pick - dot3(gp, c_all, NN)
        pd = -(dot3(hp, c_all, NT) + dot3(gp, d_all, NT) + dot3(gp, d_all, NN))
        ic, idt = dot3(factor, split(pc), TN), dot3(factor, split(pd), TN)
        inner = dot3(split(ic), hp, NT) + dot3(split(idt), gp, NT)
        coupling = dot3(split(inner), factor, NN)
        ct[at] = ic
        dt[at] = idt - 0.5 * dotf(coupling, pick, NN)

    def inner_products():
        total.finish()
        both = summed[:, :group].reshape(nv, nv)
        turned = both.T
        hmat[...] = jnp.where(below, both, turned)
        gmat[...] = jnp.where(on, summed[0, group:group + 1], jnp.where(below, turned, both))

    def coefficients():
        for p in range(panels):
            panel(p)

    right_copies = (
        pltpu.make_async_copy(yzh, zh_hbm, z_sem.at[0]), pltpu.make_async_copy(yzl, zl_hbm, z_sem.at[1]))

    def right_side():
        c_pair = split(ct[...])
        ct_pair = split(ct[...].T)
        d_pair = split(dt[...] + dt[...].T)
        for s in range(8):
            at = slice(s * lanes, (s + 1) * lanes)
            vc, yc = split(colbuf[s, :nv]), split(colbuf[s, nv:])
            zh[:, at], zl[:, at] = split(dot3(d_pair, vc, NN) + dot3(c_pair, yc, NN))
            yzh[:, at], yzl[:, at] = split(dot3(ct_pair, vc, NN))
        for copy in right_copies:
            copy.start()

    tall, wide = 4 * lanes, 2 * lanes

    def middle_copy(g):
        at = pl.ds(pl.multiple_of(g * tall, tall), tall)
        return pltpu.make_async_copy(a_mem.at[at], mid_hbm.at[at], m_sem.at[g])

    def reflector_part():
        @pl.loop(0, rows // tall)
        def _(g):
            at = pl.ds(pl.multiple_of(g * tall, tall), tall)
            left_pair = (ah[at, :nv], al[at, :nv])
            for n in range(cols // wide):
                to = slice(n * wide, (n + 1) * wide)
                a_mem[at, to] = a_mem[at, to] - dot3(left_pair, (zh[:, to], zl[:, to]), NN)
            middle_copy(g).start()

    ring_y = plane_gather(pos, yrows, ys, yr, {
        0: (total.step3, column.relay), 2: (total.step4,),
        6: (column.finish, inner_products, coefficients, right_side, reflector_part)})

    def row_copy(slot):
        b = pos.block_of(slot // 4, slot % 4)
        return pltpu.make_async_copy(yrows.at[slot], y_hbm.at[b], o_sem.at[slot])

    for slot in range(16):
        row_copy(slot).start()
    v_done()
    y_done()
    for ring in (ring_v, ring_c, ring_z, ring_y, column.ring):
        ring.drain()
    for copy in right_copies:
        copy.wait()
    for g in range(rows // tall):
        middle_copy(g).wait()
    for slot in range(16):
        row_copy(slot).wait()


def product_kernel(mid_ref, y_ref, zh, zl, out_ref):
    tile = out_ref.shape[0]
    at = pl.ds(pl.multiple_of(pl.program_id(0) * tile, tile), tile)
    out_ref[...] = mid_ref[at] - dot3(split(y_ref[at]), (zh[...], zl[...]), NN)


def shards(symmetric, reflectors, tri_factor):
    panels, nb, lanes = reflectors.shape
    nv = panels * nb
    rows, cols = symmetric.shape
    anywhere = pl.BlockSpec(memory_space=pl.ANY)
    dma = pltpu.SemaphoreType.DMA
    shape = jax.ShapeDtypeStruct
    middle, y_rows, zh, zl = pl.pallas_call(
        functools.partial(panel_kernel, panels),
        out_shape=(
            shape((rows, cols), F32), shape((16, lanes, nv), F32),
            shape((nv, cols), BF16), shape((nv, cols), BF16)),
        in_specs=[pl.BlockSpec(memory_space=pltpu.HBM)] * 3,
        out_specs=(anywhere,) * 4,
        scratch_shapes=[
            pltpu.VMEM((rows, cols), F32),
            pltpu.VMEM((rows, cols), BF16), pltpu.VMEM((rows, cols), BF16),
            pltpu.VMEM((16, nv, lanes), F32),
            pltpu.VMEM((nv, rows), BF16), pltpu.VMEM((nv, rows), BF16),
            pltpu.VMEM((8, nv, lanes), F32),
            pltpu.VMEM((4, nv, lanes), F32),
            pltpu.VMEM((2, nv // 2, lanes), F32),
            pltpu.VMEM((2, nv, lanes), F32),
            pltpu.VMEM((lanes, nv), F32),
            pltpu.VMEM((8, 2 * nv, lanes), F32),
            pltpu.VMEM((16, lanes, nv), F32),
            pltpu.VMEM((8, nv // 8 + 8, nv), F32), pltpu.VMEM((8, nv // 8 + 8, nv), F32),
            pltpu.VMEM((nv, nv), F32), pltpu.VMEM((nv, nv), F32),
            pltpu.VMEM((nv // 8 + 8, nv), F32),
            pltpu.VMEM((7, nv // 8 + 8, nv), F32),
            pltpu.VMEM((3, nv // 8 + 8, nv), F32),
            pltpu.VMEM((4, nv // 8 + 8, nv), F32),
            pltpu.VMEM((nv, nv), F32), pltpu.VMEM((nv, nv), F32),
            pltpu.VMEM((nv, cols), BF16), pltpu.VMEM((nv, cols), BF16),
            pltpu.VMEM((nv, cols), BF16), pltpu.VMEM((nv, cols), BF16),
            pltpu.VMEM(tri_factor.shape, F32),
            dma, dma((2,)), dma((4,)), dma((16,)), dma((2,)),
            dma((40,)), dma((40,)), dma((40,)), dma((40,)),
            dma((8,)), dma((8,)), dma((20,)), dma((20,)),
            dma((4,)), dma((4,)), dma((4,)), dma((4,)), dma((2,)), dma((2,)),
        ],
        compiler_params=pltpu.CompilerParams(
            collective_id=0, has_side_effects=True, vmem_limit_bytes=34 * 2**20),
    )(*(pltpu.with_memory_space_constraint(v, pltpu.HBM) for v in (symmetric, reflectors.reshape(nv, lanes), tri_factor)))
    tile = 4 * lanes
    vmem = pl.BlockSpec(memory_space=pltpu.VMEM)
    return pl.pallas_call(
        product_kernel,
        grid=(rows // tile,),
        out_shape=shape((rows, cols), F32),
        in_specs=[vmem] * 4,
        out_specs=pl.BlockSpec((tile, cols), lambda i: (i, 0)),
        compiler_params=pltpu.CompilerParams(vmem_limit_bytes=16 * 2**20),
    )(middle, y_rows.reshape(rows, nv), zh, zl)


def solution(mesh):
    placed = (P("row", "col"), P(None, None, ("row", "col")), P())
    return jax.shard_map(
        shards, mesh=mesh, in_specs=placed, out_specs=P("row", "col"), check_vma=False
    )
```

```python
import functools

import jax
import jax.numpy as jnp
from jax import lax
from jax.experimental import pallas as pl
from jax.experimental.pallas import tpu as pltpu
from jax.sharding import PartitionSpec as P

MESH = pl.DeviceIdType.MESH
F32 = jnp.float32
BF16 = jnp.bfloat16
NN = (((1,), (0,)), ((), ()))
NT = (((1,), (1,)), ((), ()))
TN = (((0,), (0,)), ((), ()))


def split(value):
    high = value.astype(BF16)
    return high, (value - high.astype(F32)).astype(BF16)


def dot3(left, right, dims):
    (lh, ll), (rh, rl) = left, right
    dot = functools.partial(lax.dot_general, dimension_numbers=dims, preferred_element_type=F32)
    return dot(lh, rh) + dot(lh, rl) + dot(ll, rh)


def dotf(left, right, dims):
    return dot3(split(left), split(right), dims)


class Place:
    def __init__(self):
        row, col = lax.axis_index("row"), lax.axis_index("col")
        self.z, self.k = row // 2, lax.rem(row, 2)
        self.y, self.x = col // 4, lax.rem(col, 4)
        self.s = row

    def dev(self, z=None, k=None, y=None, x=None):
        z = self.z if z is None else z
        k = self.k if k is None else k
        y = self.y if y is None else y
        x = self.x if x is None else x
        return (z * 2 + k, y * 4 + x)

    def out_v(self):
        s = lax.rem(self.y, 2) * 4 + self.x
        return self.dev(s // 2, lax.rem(s, 2), self.z, self.k * 2 + self.y // 2), s

    def out_y(self):
        side = 2 * lax.rem(self.x, 2) - 1
        x = lax.rem(self.x + side * self.k + 4, 4)
        y = lax.rem(self.y + self.z + 2 * self.k, 4)
        return self.dev(self.y, self.x // 2, y, x), y * 4 + x

    def from_v(self):
        b = lax.rem(self.x, 2) * 8 + self.s
        return self.dev(self.y, self.x // 2, b // 4, lax.rem(b, 4))

    def source(self, y, x):
        d = lax.rem(x - 2 * self.k + 4, 4)
        k = d // 2
        right = jnp.where(jnp.logical_or(d == 1, d == 2), 1, 0)
        z = lax.rem(y - self.z + 8 - 2 * k, 4)
        return right, z, k

    def from_y(self):
        right, z, k = self.source(self.y, self.x)
        return self.dev(z, k, self.z, 2 * self.k + right)

    def block_of(self, y, x):
        right, z, k = self.source(y, x)
        return right * 8 + 2 * z + k


def wrap(value, by):
    return lax.rem(value + by + 4, 4)


class Ring:
    def __init__(self, ssem, rsem):
        self.ssem, self.rsem = ssem, rsem
        self.sent = []

    def copy(self, i, src, dst, dev):
        return pltpu.make_async_remote_copy(
            src_ref=src, dst_ref=dst, send_sem=self.ssem.at[i], recv_sem=self.rsem.at[i],
            device_id=dev, device_id_type=MESH)

    def send(self, i, src, dst, dev):
        c = self.copy(i, src, dst, dev)
        c.start()
        self.sent.append(c)

    def got(self, i, ref, dev):
        self.copy(i, ref, ref, dev).wait_recv()

    def drain(self):
        for c in self.sent:
            c.wait_send()
        self.sent = []


def plane_gather(pos, buf, ssem, rsem, hooks=None):
    ring = Ring(ssem, rsem)
    rows = buf.shape[1]
    half, quarter = rows // 2, rows // 4
    me = pos.dev()
    direct = (3,)

    class Half:
        def __init__(self, h):
            self.h, self.base = h, h * 20
            self.i, self.j = (pos.x, pos.y) if h == 0 else (pos.y, pos.x)

        def at(self, di, dj, part=None):
            i, j = wrap(self.i, di), wrap(self.j, dj)
            slot = j * 4 + i if self.h == 0 else i * 4 + j
            if part is None:
                return buf.at[slot, pl.ds(self.h * half, half)]
            return buf.at[slot, pl.ds(self.h * half + part * quarter, quarter)]

        def first(self, d):
            return pos.dev(x=wrap(pos.x, d)) if self.h == 0 else pos.dev(y=wrap(pos.y, d))

        def second(self, d):
            return pos.dev(y=wrap(pos.y, d)) if self.h == 0 else pos.dev(x=wrap(pos.x, d))

        def send1(self):
            for n, d in ((0, 1), (1, -1)):
                ring.send(self.base + n, self.at(0, 0), self.at(0, 0), self.first(d))
            ring.send(self.base + 2, self.at(0, 0), self.at(0, 0), self.first(2))

        def relay1(self, n):
            d = (-1, 1)[n]
            ring.got(self.base + n, self.at(d, 0), me)

        def far1(self):
            ring.got(self.base + 2, self.at(2, 0), me)

        def send2(self, c):
            di = (0, -1, 1, 2)[c]
            for n, d in ((0, 1), (1, -1)):
                ring.send(self.base + 4 + 4 * c + n, self.at(di, 0), self.at(di, 0), self.second(d))
            if c in direct:
                ring.send(self.base + 6 + 4 * c, self.at(di, 0), self.at(di, 0), self.second(2))

        def relay2(self, c):
            di = (0, -1, 1, 2)[c]
            for n, d in ((0, -1), (1, 1)):
                ring.got(self.base + 4 + 4 * c + n, self.at(di, d), me)
                if c not in direct:
                    ref = self.at(di, d, n)
                    ring.send(self.base + 6 + 4 * c + n, ref, ref, self.second(-d))

        def far2(self, c):
            di = (0, -1, 1, 2)[c]
            if c in direct:
                return ring.got(self.base + 6 + 4 * c, self.at(di, 2), me)
            for n in (0, 1):
                ring.got(self.base + 6 + 4 * c + n, self.at(di, 2, n), me)

    hooks = hooks or {}
    hook = lambda n: [task() for task in hooks.get(n, ())]
    halves = (Half(0), Half(1))
    for h in halves:
        h.send1()
    for h in halves:
        h.send2(0)
    hook(0)
    for n in (0, 1):
        for h in halves:
            h.relay1(n)
            h.send2(1 + n)
    hook(1)
    for h in halves:
        h.far1()
        h.send2(3)
    hook(2)
    for h in halves:
        h.relay2(0)
    hook(3)
    for c in (1, 2, 3):
        for h in halves:
            h.relay2(c)
        hook(3 + c)
    for c in (0, 1, 2, 3):
        for h in halves:
            h.far2(c)
    return ring


class Column:
    def __init__(self, pos, buf, ssem, rsem):
        self.pos, self.buf = pos, buf
        self.ring = Ring(ssem, rsem)
        self.me = pos.dev()
        self.partner = pos.dev(k=1 - pos.k)
        self.quarter = buf.shape[1] // 2

    def at(self, dz, part=None, other=False):
        k = 1 - self.pos.k if other else self.pos.k
        slot = wrap(self.pos.z, dz) * 2 + k
        if part is None:
            return self.buf.at[slot]
        return self.buf.at[slot, pl.ds(part * self.quarter, self.quarter)]

    def zdev(self, d):
        return self.pos.dev(z=wrap(self.pos.z, d))

    def start(self):
        own = self.at(0)
        self.ring.send(0, own, own, self.zdev(1))
        self.ring.send(1, own, own, self.zdev(-1))
        self.ring.send(4, own, own, self.partner)

    def relay(self):
        for n, d in ((0, -1), (1, 1)):
            ref = self.at(d)
            self.ring.got(n, ref, self.me)
            part = self.at(d, n)
            self.ring.send(2 + n, part, part, self.zdev(-d))
            self.ring.send(5 + n, ref, ref, self.partner)

    def finish(self):
        for n in (0, 1):
            self.ring.got(2 + n, self.at(2, n), self.me)
        ref = self.at(2)
        self.ring.send(7, ref, ref, self.partner)
        for i, dz in ((4, 0), (5, -1), (6, 1), (7, 2)):
            self.ring.got(i, self.at(dz, other=True), self.me)


class Total:
    def __init__(self, pos, whole, out, part, in1, in2, in3, ssem, rsem):
        self.pos, self.whole, self.out, self.part = pos, whole, out, part
        self.ins = (in1, in2, in3)
        self.ring = Ring(ssem, rsem)
        self.me = pos.dev()

    def other(self, d):
        s = lax.rem(self.pos.s + d, 8)
        return s, self.pos.dev(s // 2, lax.rem(s, 2))

    def piece(self, s, ref=None):
        ref = self.whole if ref is None else ref
        return ref.at[s]

    def step1(self):
        for d in range(1, 8):
            s, dev = self.other(d)
            self.ring.send(d - 1, self.piece(s), self.ins[0].at[d - 1], dev)

    def step2(self):
        value = self.piece(self.pos.s)[...]
        for d in range(7):
            self.ring.got(d, self.ins[0].at[d], self.me)
            value = value + self.ins[0][d]
        self.part[...] = value
        for d in (1, 2, 3):
            self.ring.send(6 + d, self.part, self.ins[1].at[d - 1], self.pos.dev(x=wrap(self.pos.x, d)))

    def step3(self):
        value = self.part[...]
        for d in (1, 2, 3):
            self.ring.got(6 + d, self.ins[1].at[d - 1], self.me)
            value = value + self.ins[1][d - 1]
        mid = self.ins[2].at[3]
        mid[...] = value
        for d in (1, 2, 3):
            self.ring.send(9 + d, mid, self.ins[2].at[d - 1], self.pos.dev(y=wrap(self.pos.y, d)))

    def step4(self):
        value = self.ins[2][3]
        for d in (1, 2, 3):
            self.ring.got(9 + d, self.ins[2].at[d - 1], self.me)
            value = value + self.ins[2][d - 1]
        own = self.piece(self.pos.s, self.out)
        own[...] = value
        for d in range(1, 8):
            _, dev = self.other(d)
            self.ring.send(12 + d, own, own, dev)

    def finish(self):
        for d in range(1, 8):
            s, _ = self.other(8 - d)
            self.ring.got(12 + d, self.piece(s, self.out), self.me)
        self.ring.drain()


def exchange(dev, me, src, dst, ssem, rsem):
    here = jnp.logical_and(dev[0] == me[0], dev[1] == me[1])
    remote = pltpu.make_async_remote_copy(
        src_ref=src, dst_ref=dst, send_sem=ssem, recv_sem=rsem, device_id=dev, device_id_type=MESH)

    @pl.when(here)
    def _():
        pltpu.make_async_copy(src, dst, rsem).start()

    @pl.when(jnp.logical_not(here))
    def _():
        remote.start()

    def drain():
        @pl.when(jnp.logical_not(here))
        def _():
            remote.wait_send()

    return drain


def panel_kernel(
    panels, a_hbm, v_hbm, tri_hbm, mid_hbm, y_hbm, zh_hbm, zl_hbm,
    a_mem, ah, al, vbuf, vh, vl, pbuf, cin, rin1, rin2, ytr, colbuf, yrows,
    packed, summed, gmat, hmat, part, tin1, tin2, tin3, ct, dt, zh, zl, yzh, yzl, tri_ref,
    a_sem, in_sem, m_sem, o_sem, z_sem, vs, vr, ys, yr, cols_s, cols_r, hs, hr, cs, cr, zs, zr, ts, tr,
):
    pos = Place()
    me = pos.dev()
    own = pos.y * 4 + pos.x
    v_ref = vbuf.at[own]
    nv, lanes = v_ref.shape
    nb = nv // panels
    rows, cols = a_mem.shape
    small = (
        pltpu.make_async_copy(v_hbm, v_ref, in_sem.at[0]), pltpu.make_async_copy(tri_hbm, tri_ref, in_sem.at[1]))
    for copy in small:
        copy.start()
    load = pltpu.make_async_copy(a_hbm, a_mem, a_sem)
    load.start()

    v_to, v_slot = pos.out_v()
    y_to, y_slot = pos.out_y()

    barrier = pltpu.get_barrier_semaphore()
    near = [pos.dev(x=wrap(pos.x, d)) for d in (1, 2, 3)]
    near += [pos.dev(y=wrap(pos.y, d)) for d in (1, 2, 3)]
    for d in range(1, 8):
        s = lax.rem(pos.s + d, 8)
        near.append(pos.dev(s // 2, lax.rem(s, 2)))
    near += [pos.from_v(), pos.from_y()]
    for dev in near:
        pl.semaphore_signal(barrier, inc=1, device_id=dev, device_id_type=MESH)
    for copy in small:
        copy.wait()
    pl.semaphore_wait(barrier, len(near))

    def pairs():
        load.wait()

        @pl.loop(0, rows // lanes)
        def _(i):
            at = pl.ds(pl.multiple_of(i * lanes, lanes), lanes)
            ah[at], al[at] = split(a_mem[at])

    ring_v = plane_gather(pos, vbuf, vs, vr, {6: (pairs,)})
    for b in range(16):
        high, low = split(vbuf[b])
        vh[:, b * lanes:(b + 1) * lanes] = high
        vl[:, b * lanes:(b + 1) * lanes] = low

    ring_c, ring_z = Ring(cs, cr), Ring(zs, zr)
    partner = pos.dev(k=1 - pos.k)
    half = nv // 2
    far, right, left = wrap(pos.z, 2), wrap(pos.z, 1), wrap(pos.z, -1)
    order = (far, right, left, pos.z)

    def product(i):
        at = pl.ds(pl.multiple_of(order[i] * 2 * lanes, 2 * lanes), 2 * lanes)
        value = dot3((vh[...], vl[...]), (ah[:, at], al[:, at]), NN)
        pbuf[2 * i] = value[:, :lanes]
        pbuf[2 * i + 1] = value[:, lanes:]
        ring_c.send(i, pbuf.at[2 * i + 1 - pos.k], cin.at[i], partner)

    def merge(i):
        ring_c.got(i, cin.at[i], me)
        cin[i] = cin[i] + pbuf[2 * i + pos.k]

    product(0)
    v_done = exchange(v_to, me, v_ref, colbuf.at[v_slot, pl.ds(0, nv)], ts.at[0], tr.at[0])
    product(1)
    merge(0)
    ring_z.send(0, cin.at[0, pl.ds(0, half)], rin1.at[0], pos.dev(z=right))
    ring_z.send(1, cin.at[0, pl.ds(half, half)], rin1.at[1], pos.dev(z=left))
    product(2)
    product(3)
    for n, to in ((0, right), (1, left)):
        merge(1 + n)
        ring_z.got(n, rin1.at[n], me)
        at = cin.at[1 + n, pl.ds(n * half, half)]
        at[...] = at[...] + rin1[n]
        ring_z.send(2 + n, cin.at[1 + n], rin2.at[n], pos.dev(z=to))
    merge(3)
    for n in (0, 1):
        ring_z.got(2 + n, rin2.at[n], me)
    shard = cin[3] + rin2[0] + rin2[1]
    ytr[...] = shard.T
    y_done = exchange(y_to, me, ytr, yrows.at[y_slot], ts.at[1], tr.at[1])
    colbuf[pos.s, nv:] = shard

    own_v = colbuf.at[pos.s, pl.ds(0, nv)]
    pltpu.make_async_copy(own_v, own_v, tr.at[0]).wait()
    row = lax.broadcasted_iota(jnp.int32, (nv, nv), 0)
    column_index = lax.broadcasted_iota(jnp.int32, (nv, nv), 1)
    below, on = row >= column_index, row == column_index
    group = nv // 8
    gram = dotf(v_ref[...], v_ref[...], NT)
    packed[:, group:] = jnp.zeros_like(packed[:, group:])
    packed[:, :group] = jnp.where(below, dotf(own_v[...], shard, NT), gram).reshape(8, group, nv)
    packed[0, group:group + 1] = jnp.sum(jnp.where(on, gram, 0.0), axis=0, keepdims=True)
    total = Total(pos, packed, summed, part, tin1, tin2, tin3, hs, hr)
    total.step1()
    column = Column(pos, colbuf, cols_s, cols_r)
    column.start()

    @pl.loop(0, 16)
    def _(b):
        at = pl.ds(pl.multiple_of(b * lanes, lanes), lanes)
        ah[at, :nv], al[at, :nv] = split(vbuf[b].T)

    total.step2()
    own_y = yrows.at[pos.y * 4 + pos.x]
    pltpu.make_async_copy(own_y, own_y, tr.at[1]).wait()

    ct[...] = jnp.zeros_like(ct)
    dt[...] = jnp.zeros_like(dt)

    def panel(p):
        at = pl.ds(p * nb, nb)
        factor = split(tri_ref[p])
        pick = (lax.broadcasted_iota(jnp.int32, (nb, nv), 1)
                == lax.broadcasted_iota(jnp.int32, (nb, nv), 0) + p * nb).astype(F32)
        gp, hp = split(gmat[at]), split(hmat[at])
        c_all, d_all = split(ct[...]), split(dt[...])
        pc = pick - dot3(gp, c_all, NN)
        pd = -(dot3(hp, c_all, NT) + dot3(gp, d_all, NT) + dot3(gp, d_all, NN))
        ic, idt = dot3(factor, split(pc), TN), dot3(factor, split(pd), TN)
        inner = dot3(split(ic), hp, NT) + dot3(split(idt), gp, NT)
        coupling = dot3(split(inner), factor, NN)
        ct[at] = ic
        dt[at] = idt - 0.5 * dotf(coupling, pick, NN)

    def inner_products():
        total.finish()
        both = summed[:, :group].reshape(nv, nv)
        turned = both.T
        hmat[...] = jnp.where(below, both, turned)
        gmat[...] = jnp.where(on, summed[0, group:group + 1], jnp.where(below, turned, both))

    def coefficients():
        for p in range(panels):
            panel(p)

    right_copies = (
        pltpu.make_async_copy(yzh, zh_hbm, z_sem.at[0]), pltpu.make_async_copy(yzl, zl_hbm, z_sem.at[1]))

    def right_side():
        c_pair = split(ct[...])
        ct_pair = split(ct[...].T)
        d_pair = split(dt[...] + dt[...].T)
        for s in range(8):
            at = slice(s * lanes, (s + 1) * lanes)
            vc, yc = split(colbuf[s, :nv]), split(colbuf[s, nv:])
            zh[:, at], zl[:, at] = split(dot3(d_pair, vc, NN) + dot3(c_pair, yc, NN))
            yzh[:, at], yzl[:, at] = split(dot3(ct_pair, vc, NN))
        for copy in right_copies:
            copy.start()

    tall, wide = 4 * lanes, 2 * lanes

    def middle_copy(g):
        at = pl.ds(pl.multiple_of(g * tall, tall), tall)
        return pltpu.make_async_copy(a_mem.at[at], mid_hbm.at[at], m_sem.at[g])

    def reflector_part():
        @pl.loop(0, rows // tall)
        def _(g):
            at = pl.ds(pl.multiple_of(g * tall, tall), tall)
            left_pair = (ah[at, :nv], al[at, :nv])
            for n in range(cols // wide):
                to = slice(n * wide, (n + 1) * wide)
                a_mem[at, to] = a_mem[at, to] - dot3(left_pair, (zh[:, to], zl[:, to]), NN)
            middle_copy(g).start()

    ring_y = plane_gather(pos, yrows, ys, yr, {
        0: (total.step3, column.relay), 2: (total.step4,),
        6: (column.finish, inner_products, coefficients, right_side, reflector_part)})

    def row_copy(slot):
        b = pos.block_of(slot // 4, slot % 4)
        return pltpu.make_async_copy(yrows.at[slot], y_hbm.at[b], o_sem.at[slot])

    for slot in range(16):
        row_copy(slot).start()
    v_done()
    y_done()
    for ring in (ring_v, ring_c, ring_z, ring_y, column.ring):
        ring.drain()
    for copy in right_copies:
        copy.wait()
    for g in range(rows // tall):
        middle_copy(g).wait()
    for slot in range(16):
        row_copy(slot).wait()


def product_kernel(mid_ref, y_ref, zh, zl, out_ref):
    tile = out_ref.shape[0]
    at = pl.ds(pl.multiple_of(pl.program_id(0) * tile, tile), tile)
    out_ref[...] = mid_ref[at] - dot3(split(y_ref[at]), (zh[...], zl[...]), NN)


def shards(symmetric, reflectors, tri_factor):
    panels, nb, lanes = reflectors.shape
    nv = panels * nb
    rows, cols = symmetric.shape
    anywhere = pl.BlockSpec(memory_space=pl.ANY)
    dma = pltpu.SemaphoreType.DMA
    shape = jax.ShapeDtypeStruct
    middle, y_rows, zh, zl = pl.pallas_call(
        functools.partial(panel_kernel, panels),
        out_shape=(
            shape((rows, cols), F32), shape((16, lanes, nv), F32),
            shape((nv, cols), BF16), shape((nv, cols), BF16)),
        in_specs=[pl.BlockSpec(memory_space=pltpu.HBM)] * 3,
        out_specs=(anywhere,) * 4,
        scratch_shapes=[
            pltpu.VMEM((rows, cols), F32),
            pltpu.VMEM((rows, cols), BF16), pltpu.VMEM((rows, cols), BF16),
            pltpu.VMEM((16, nv, lanes), F32),
            pltpu.VMEM((nv, rows), BF16), pltpu.VMEM((nv, rows), BF16),
            pltpu.VMEM((8, nv, lanes), F32),
            pltpu.VMEM((4, nv, lanes), F32),
            pltpu.VMEM((2, nv // 2, lanes), F32),
            pltpu.VMEM((2, nv, lanes), F32),
            pltpu.VMEM((lanes, nv), F32),
            pltpu.VMEM((8, 2 * nv, lanes), F32),
            pltpu.VMEM((16, lanes, nv), F32),
            pltpu.VMEM((8, nv // 8 + 8, nv), F32), pltpu.VMEM((8, nv // 8 + 8, nv), F32),
            pltpu.VMEM((nv, nv), F32), pltpu.VMEM((nv, nv), F32),
            pltpu.VMEM((nv // 8 + 8, nv), F32),
            pltpu.VMEM((7, nv // 8 + 8, nv), F32),
            pltpu.VMEM((3, nv // 8 + 8, nv), F32),
            pltpu.VMEM((4, nv // 8 + 8, nv), F32),
            pltpu.VMEM((nv, nv), F32), pltpu.VMEM((nv, nv), F32),
            pltpu.VMEM((nv, cols), BF16), pltpu.VMEM((nv, cols), BF16),
            pltpu.VMEM((nv, cols), BF16), pltpu.VMEM((nv, cols), BF16),
            pltpu.VMEM(tri_factor.shape, F32),
            dma, dma((2,)), dma((4,)), dma((16,)), dma((2,)),
            dma((40,)), dma((40,)), dma((40,)), dma((40,)),
            dma((8,)), dma((8,)), dma((20,)), dma((20,)),
            dma((4,)), dma((4,)), dma((4,)), dma((4,)), dma((2,)), dma((2,)),
        ],
        compiler_params=pltpu.CompilerParams(
            collective_id=0, has_side_effects=True, vmem_limit_bytes=34 * 2**20),
    )(*(pltpu.with_memory_space_constraint(v, pltpu.HBM) for v in (symmetric, reflectors.reshape(nv, lanes), tri_factor)))
    tile = 4 * lanes
    vmem = pl.BlockSpec(memory_space=pltpu.VMEM)
    return pl.pallas_call(
        product_kernel,
        grid=(rows // tile,),
        out_shape=shape((rows, cols), F32),
        in_specs=[vmem] * 4,
        out_specs=pl.BlockSpec((tile, cols), lambda i: (i, 0)),
        compiler_params=pltpu.CompilerParams(vmem_limit_bytes=16 * 2**20),
    )(middle, y_rows.reshape(rows, nv), zh, zl)


def solution(mesh):
    placed = (P("row", "col"), P(None, None, ("row", "col")), P())
    return jax.shard_map(
        shards, mesh=mesh, in_specs=placed, out_specs=P("row", "col"), check_vma=False
    )
```
